512 devices in a mesh: shard: 128 (over y, z, core), rep: 4 (over x).
Axes of the slice: x: 4, y: 8, z: 8, core: 2. Of those that a mesh axis runs over, the one named last changes fastest.
Arguments:
- memory: bfloat16 [131072, 512], P('shard'), may hold values from -4 to 4
- touch_owner: int32 [131072, 1], P(('shard', 'rep')), may hold values from 0 to 127; in each aligned block of 256 rows (0 to 255, 256 to 511, ...) at most 6 rows name the same one
- touch_row: int32 [131072], P(('shard', 'rep')), may hold values from 0 to 1023
- touch_time: int32 [131072], P(('shard', 'rep')), may hold values from 0 to 999
- src_slot: int32 [196608], P(('shard', 'rep')), may hold values from 0 to 255
- dst_slot: int32 [196608], P(('shard', 'rep')), may hold values from 0 to 255
- event_time: int32 [196608], P(('shard', 'rep')), may hold values from 1000 to 1999
- neighbour_blocks: int32 [1536, 2], P(('shard', 'rep')), may hold values from 0 to 2
- time_freq: float32 [128], replicated, may hold values from 0.001 to 1
- time_phase: float32 [128], replicated, may hold values from -3.140625 to 3.140625
- w_input: bfloat16 [512, 1536], P(None, 'rep'), may hold values from -0.25 to 0.25
- w_time: bfloat16 [128, 1536], P(None, 'rep'), may hold values from -0.5 to 0.5
- w_hidden: bfloat16 [512, 1536], P(None, 'rep'), may hold values from -0.25 to 0.25
- w_query: bfloat16 [512, 512], P(None, 'rep'), may hold values from -0.25 to 0.25
- w_keyval: bfloat16 [512, 1024], P(None, 'rep'), may hold values from -0.25 to 0.25
Outputs:
- event_embed: bfloat16 [196608, 512], P(('shard', 'rep'))
- new_memory: bfloat16 [131072, 512], P('shard')
The draws below stay inside these ranges and needn't reach their ends.
Inputs may be any that keep to these rules, and one draw needn't show every extreme that they name: `touch_owner`: in each batch of 256 touched entries at most 6 have the same owner, and some owner has exactly 6 in every draw.
All inputs are finite; a program needn't handle non-finite values.
Results may differ from the reference program's by a relative error of at most 0.0054.
Values may be sent and summed in bfloat16 or wider, within the bound.
A program may use at most 64 MiB of HBM per device.

```python
import math
import jax
import jax.numpy as jnp
import numpy as np
from jax import lax

D = 512
TD = 128
H = 4
BLK = 128
NB = 2
EV_DEV = 384
TOUCH = 256
ROWS_DEV = 1024
CAP = 6
QBLK = 3
EVENTS = 196608
TOUCHES = 131072
QBLOCKS = 1536
VERT = 131072
N_SHARD = 128
N_REP = 4


def touch_ends(values, rng, smallest, largest):
    place = [jax.random.randint(jax.random.fold_in(rng, axis), (), 0, length) for axis, length in enumerate(values.shape)]
    widest = values.shape.index(max(values.shape))
    beside = place[:widest] + [(place[widest] + 1) % values.shape[widest]] + place[widest + 1:]
    return values.at[tuple(place)].set(smallest).at[tuple(beside)].set(largest)


def levels(stream_key, extent, pieces, least, high):
    factor_of = 1.0
    for axis_at, blocks in pieces:
        draws = jax.random.uniform(jax.random.fold_in(jax.random.fold_in(stream_key, 6), axis_at), (blocks,), jnp.float32, least / len(pieces), high / len(pieces))
        factor_of = factor_of * jnp.repeat(jnp.exp(draws), extent[axis_at] // blocks).reshape((-1,) + (1,) * (len(extent) - 1 - axis_at))
    return factor_of


def assign_block(stream_key, own, number, rows, amount, top, bound, slope):
    order = jax.random.permutation(stream_key, amount)
    crowded, common = load_shares(amount, rows * top, bound, slope, True), load_shares(amount, rows * top, bound, slope, False)
    places = jnp.arange(amount)

    def named(lengths, turn):
        used = int((lengths > 0).sum())
        fixed = max(1, used // 4)
        shifted = fixed + (places - fixed + turn * (used - fixed)) % max(1, amount - fixed)
        return jnp.zeros((amount,), jnp.int32).at[order[jnp.where(places < fixed, places, shifted)]].set(jnp.asarray(lengths, jnp.int32))

    lengths = jnp.where(number % 4 == 0, named(crowded, number // 4), named(common, number - number // 4 - 1))
    mixed = jax.random.permutation(jax.random.fold_in(own, 3), amount)
    giver, taker = mixed[0:amount // 2 * 2:2], mixed[1:amount // 2 * 2:2]
    margin = jnp.minimum(lengths[giver] - 1, bound - lengths[taker]) // 2
    margin = jnp.where((giver == order[0]) | (taker == order[0]) | (lengths[taker] == 0), 0, jnp.maximum(margin, 0))
    shifted = jax.random.randint(jax.random.fold_in(own, 4), (amount // 2,), 0, 1 << 20) % (margin + 1)
    lengths = lengths.at[giver].add(-shifted).at[taker].add(shifted)
    items = jnp.searchsorted(jnp.cumsum(lengths), jnp.arange(rows * top), side="right").astype(jnp.int32)
    grid = items.reshape(top, rows).T
    grid = grid[jax.random.permutation(jax.random.fold_in(own, 1), rows)]
    turn = jax.random.randint(jax.random.fold_in(own, 2), (rows, 1), 0, top)
    return jnp.take_along_axis(grid, (jnp.arange(top)[None, :] + turn) % top, axis=1)


def load_shares(number_of, total, limit, lean, full):
    weights = [(1 << 20) // math.isqrt(grade ** lean) + 1 for grade in range(1, number_of + 1)]
    largest = limit if full else min(limit, max(-(-total // number_of), total * weights[0] // sum(weights)))
    least = 1 if total - largest >= number_of - 1 else 0
    given, spare = [largest] + [least] * (number_of - 1), total - largest - least * (number_of - 1)
    while spare > 0:
        movable = [i for i in range(1, number_of) if given[i] < largest] or [i for i in range(1, number_of) if given[i] < limit]
        mass, left = sum([weights[i] for i in movable]), spare
        for i in movable:
            addition = min(limit - given[i], max(1, left * weights[i] // mass), spare)
            given[i] = given[i] + addition
            spare = spare - addition
    return np.array(given)


def gaussian(own_key, shape, deviation, bound, pieces=(), dtype=jnp.bfloat16):
    result = deviation * jax.random.normal(own_key, shape, jnp.float32)
    if pieces:
        result = result * levels(own_key, shape, pieces, -0.22, 0.18)
    return jnp.clip(result, -bound, bound).astype(dtype)


def setup_inputs(seed: int = 0) -> dict:
    splits = jax.random.split(jax.random.key(seed), 16)
    memory = gaussian(splits[0], (VERT, D), 1.0, 4.0, ((0, 128),))
    touch_owner_keys = jax.random.split(jax.random.fold_in(splits[1], 1), TOUCHES // TOUCH)
    touch_owner_turns = jax.random.permutation(jax.random.fold_in(splits[1], 3), TOUCHES // TOUCH)
    touch_owner = jax.vmap(lambda own, number: assign_block(jax.random.fold_in(splits[1], 2), own, number, TOUCH, N_SHARD, 1, CAP, 2))(touch_owner_keys, touch_owner_turns).reshape((TOUCHES, 1))
    touch_row = touch_ends(jax.random.randint(splits[2], (TOUCHES,), 0, ROWS_DEV), jax.random.fold_in(splits[2], 1), 0, ROWS_DEV - 1).astype(jnp.int32)
    touch_time = touch_ends(jax.random.randint(splits[3], (TOUCHES,), 0, 1000), jax.random.fold_in(splits[3], 1), 0, 999).astype(jnp.int32)
    src_slot = touch_ends(jax.random.randint(splits[4], (EVENTS,), 0, TOUCH), jax.random.fold_in(splits[4], 1), 0, TOUCH - 1).astype(jnp.int32)
    dst_slot = touch_ends(jax.random.randint(splits[5], (EVENTS,), 0, TOUCH), jax.random.fold_in(splits[5], 1), 0, TOUCH - 1).astype(jnp.int32)
    event_time = touch_ends(jax.random.randint(splits[6], (EVENTS,), 1000, 2000), jax.random.fold_in(splits[6], 1), 1000, 1999).astype(jnp.int32)
    neighbour_blocks = touch_ends(jax.random.randint(splits[7], (QBLOCKS, NB), 0, QBLK), jax.random.fold_in(splits[7], 1), 0, QBLK - 1).astype(jnp.int32)
    time_freq = jnp.clip(jnp.exp(jax.random.uniform(splits[8], (TD,), jnp.float32, math.log(0.001), math.log(1.0))), 0.001, 1.0)
    time_phase = jnp.clip(jax.random.uniform(splits[9], (TD,), jnp.float32, -3.140625, 3.140625), -3.140625, 3.140625)
    w_input = gaussian(splits[10], (D, 3 * D), D ** -0.5, 0.25, ((1, 4),))
    w_time = gaussian(splits[11], (TD, 3 * D), TD ** -0.5, 0.5, ((1, 4),))
    w_hidden = gaussian(splits[12], (D, 3 * D), D ** -0.5, 0.25, ((1, 4),))
    w_query = gaussian(splits[13], (D, D), D ** -0.5, 0.25, ((1, 4),))
    w_keyval = gaussian(splits[14], (D, 2 * D), D ** -0.5, 0.25, ((1, 4),))
    return dict(memory=memory, touch_owner=touch_owner, touch_row=touch_row, touch_time=touch_time, src_slot=src_slot, dst_slot=dst_slot, event_time=event_time, neighbour_blocks=neighbour_blocks, time_freq=time_freq, time_phase=time_phase, w_input=w_input, w_time=w_time, w_hidden=w_hidden, w_query=w_query, w_keyval=w_keyval)


def event_update(fetched, tick, source, target, stamp, listed, time_freq, time_phase, w_input, w_time, w_hidden, w_query, w_keyval):
    width = fetched.shape[1]
    count = stamp.shape[0]
    hsrc = fetched[source]
    hdst = fetched[target]
    spans = (stamp - tick[source]).astype(jnp.float32)
    encode = jnp.cos(spans[:, None] * time_freq[None, :] + time_phase[None, :]).astype(jnp.bfloat16)
    gin = jnp.dot(hdst, w_input, preferred_element_type=jnp.float32) + jnp.dot(encode, w_time, preferred_element_type=jnp.float32)
    ghid = jnp.dot(hsrc, w_hidden, preferred_element_type=jnp.float32)
    reset = jax.nn.sigmoid(gin[:, :width] + ghid[:, :width])
    update = jax.nn.sigmoid(gin[:, width:2 * width] + ghid[:, width:2 * width])
    fresh = jnp.tanh(gin[:, 2 * width:] + reset * ghid[:, 2 * width:])
    hold = hsrc.astype(jnp.float32)
    hnew = (1.0 - update) * fresh + update * hold
    entries = fetched.shape[0]
    counts = jax.ops.segment_sum(jnp.ones((count,), jnp.float32), source, entries)
    delta = jax.ops.segment_sum(hnew - hold, source, entries) / jnp.maximum(counts, 1.0)[:, None]
    hround = hnew.astype(jnp.bfloat16)
    query = jnp.dot(hround, w_query, preferred_element_type=jnp.float32).astype(jnp.bfloat16)
    keyval = jnp.dot(hdst, w_keyval, preferred_element_type=jnp.float32).astype(jnp.bfloat16)
    blocks = count // BLK
    headsz = width // H
    query4 = query.reshape(blocks, BLK, H, headsz)
    keys = keyval[:, :width].reshape(blocks, BLK, H, headsz)[listed].reshape(blocks, NB * BLK, H, headsz)
    values = keyval[:, width:].reshape(blocks, BLK, H, headsz)[listed].reshape(blocks, NB * BLK, H, headsz)
    scores = jnp.einsum('qihd,qjhd->qhij', query4.astype(jnp.float32), keys.astype(jnp.float32)) / math.sqrt(headsz)
    prob = jax.nn.softmax(scores, axis=-1).astype(jnp.bfloat16)
    attend = jnp.einsum('qhij,qjhd->qihd', prob.astype(jnp.float32), values.astype(jnp.float32)).reshape(count, width)
    embed = (hnew + attend).astype(jnp.bfloat16)
    return (embed, delta)

def reference(memory, touch_owner, touch_row, touch_time, src_slot, dst_slot, event_time, neighbour_blocks, time_freq, time_phase, w_input, w_time, w_hidden, w_query, w_keyval):
    batches = N_SHARD * N_REP
    vertex = (touch_owner[:, 0] * ROWS_DEV + touch_row).astype(jnp.int32)

    def one_batch(items):
        ids, tick, source, target, stamp, listed = items
        fetched = jnp.take(memory, ids, axis=0)
        return event_update(fetched, tick, source, target, stamp, listed, time_freq, time_phase, w_input, w_time, w_hidden, w_query, w_keyval)
    items = (vertex.reshape(batches, TOUCH), touch_time.reshape(batches, TOUCH), src_slot.reshape(batches, EV_DEV), dst_slot.reshape(batches, EV_DEV), event_time.reshape(batches, EV_DEV), neighbour_blocks.reshape(batches, QBLK, NB))
    embeds, deltas = lax.map(one_batch, items)
    width = memory.shape[1]
    total = jax.ops.segment_sum(deltas.reshape(-1, width), vertex, VERT)
    new_memory = (memory.astype(jnp.float32) + total).astype(jnp.bfloat16)
    return (embeds.reshape(-1, width), new_memory)
```

```python
import functools
import math

import jax
import jax.numpy as jnp
from jax import lax
from jax.experimental import pallas as pl
from jax.experimental.pallas import tpu as pltpu
from jax.sharding import PartitionSpec as P

H = 4
BLK = 128
LANES = 128
PAD = 8
F32 = jnp.float32
BF16 = jnp.bfloat16
I32 = jnp.int32


def mm(a, b):
    return jnp.dot(a, b, preferred_element_type=F32)


def mm_nt(a, b):
    return lax.dot_general(a, b, (((1,), (1,)), ((), ())), preferred_element_type=F32)


def mm_tn(a, b):
    return lax.dot_general(a, b, (((0,), (0,)), ((), ())), preferred_element_type=F32)


def iota(shape, dim):
    return lax.broadcasted_iota(I32, shape, dim)


def one_hot(cond):
    return jnp.where(cond, 1.0, 0.0).astype(BF16)


def column(row):
    return jnp.transpose(jnp.broadcast_to(row, (LANES, row.shape[1])))


def rowhot(col, width):
    lane = iota(col.shape, 1).astype(F32)
    parts = [one_hot(col == lane + float(k * LANES)) for k in range(pl.cdiv(width, LANES))]
    hot = parts[0] if len(parts) == 1 else jnp.concatenate(parts, axis=1)
    return hot if hot.shape[1] == width else hot[:, :width]


def body(
    n, m, cap,
    owner_ref, row_ref, tick_ref, src_ref, dst_ref, stamp_ref, listed_ref, freq_ref, phase_ref,
    mem_hbm, wi_hbm, wt_hbm, wh_hbm, wq_hbm, wk_hbm,
    embed_ref, new_ref,
    mem, wi, wt, wh, wq, wk,
    reqbuf, asked, asked_all, slots_all, served, rows, place_hot, owner_hot,
    hs, hd, hn, dsend, dall, outbuf, landed, newcol,
    local_sem, req_sem, slot_sem, ask_sem, wx_sem, wc_sem, row_sem, delta_sem, out_sem, new_sem,
):
    s = lax.axis_index("shard")
    r = lax.axis_index("rep")
    T = owner_ref.shape[1]
    E = src_ref.shape[0]
    R, D = mem.shape
    G = m * cap
    core = lax.rem(s, 2)
    sibling = s + 1 - 2 * core

    def plane(i):
        return lax.rem(s + i, n)

    def line(i):
        return lax.rem(r + i, m)

    def remote(src, dst, sems, at, shard, rep):
        return pltpu.make_async_remote_copy(
            src_ref=src, dst_ref=dst, send_sem=sems.at[(0,) + at], recv_sem=sems.at[(1,) + at],
            device_id=(shard, rep), device_id_type=pl.DeviceIdType.MESH,
        )

    def finish(ref, sem):
        pltpu.make_async_copy(ref, ref, sem).wait()

    weights = ((wi_hbm, wi), (wt_hbm, wt), (wh_hbm, wh), (wq_hbm, wq), (wk_hbm, wk))
    mem_copy = pltpu.make_async_copy(mem_hbm, mem, local_sem.at[0])
    mem_copy.start()
    own = []
    for at, (shard_ref, full) in enumerate(weights):
        width = shard_ref.shape[1]
        copy = pltpu.make_async_copy(
            shard_ref, full.at[:, pl.ds(pl.multiple_of(r * width, LANES), width)], local_sem.at[1 + at]
        )
        copy.start()
        own.append(copy)

    barrier = pltpu.get_barrier_semaphore()

    def greet(i, carry):
        pl.semaphore_signal(barrier, inc=1, device_id=(plane(i), r), device_id_type=pl.DeviceIdType.MESH)
        return carry

    lax.fori_loop(1, n, greet, 0)
    for i in range(1, m):
        pl.semaphore_signal(barrier, inc=1, device_id=(s, line(i)), device_id_type=pl.DeviceIdType.MESH)

    owner = owner_ref[...]
    hit = one_hot(iota((n, T), 0) == owner)
    earlier = one_hot(iota((T, T), 0) < iota((T, T), 1))
    place = jnp.sum(mm(hit, earlier) * hit.astype(F32), axis=0, keepdims=True)
    asked_row = row_ref[...] + 1
    line_at = iota((LANES, T), 0).astype(F32)
    ask_hi = (asked_row >> 5).astype(F32)
    ask_lo = (asked_row & 31).astype(F32)
    table = jnp.where(line_at == place, ask_hi, jnp.where(line_at == place + float(PAD), ask_lo, 0.0))
    reqbuf[...] = mm_nt(hit, table.astype(BF16)).reshape(n, 1, LANES)
    ownerf = owner.astype(F32)
    slots_all[r] = ownerf * float(G) + place + (r * cap).astype(F32)
    asked[s] = reqbuf[s]

    pl.semaphore_wait(barrier, n - 1 + m - 1)

    def ask(i, carry):
        to = plane(i)
        remote(reqbuf.at[to], asked.at[s], req_sem, (), to, r).start()
        return carry

    lax.fori_loop(1, n, ask, 0)
    for i in range(1, m):
        remote(slots_all.at[r], slots_all.at[r], slot_sem, (i,), s, line(i)).start()

    def halves(group):
        out = []
        for w in group:
            shard_ref, full = weights[w]
            depth, width = shard_ref.shape
            half = depth // 2
            out.append((w, shard_ref, full, pl.ds(pl.multiple_of(core * half, PAD), half), width))
        return out

    groups = ((1, 2, 0), (3, 4))
    for group in groups:
        for i in range(1, m):
            for w, shard_ref, full, part, width in halves(group):
                cols = pl.ds(pl.multiple_of(r * width, LANES), width)
                remote(shard_ref.at[part], full.at[part, cols], wx_sem, (w, i), s, line(i)).start()

    finish(asked.at[pl.ds(0, n - 1)], req_sem.at[1])
    table_in = asked[...].reshape(n, LANES)
    asked_all[r] = table_in
    for i in range(1, m):
        remote(asked_all.at[r], asked_all.at[r], ask_sem, (i,), s, line(i)).start()
    spread = one_hot((iota((n * PAD, n), 0) >> 3) == iota((n * PAD, n), 1))
    lane = iota((n * PAD, LANES), 1)
    mine = ((lane & (PAD - 1)) == (iota((n * PAD, LANES), 0) & (PAD - 1))) & (lane < 2 * PAD)
    picked = jnp.where(mine, mm(spread, table_in.astype(BF16)), 0.0).astype(BF16)
    depth_at = iota((LANES, LANES), 0)
    scale = jnp.where(depth_at < PAD, 32.0, jnp.where(depth_at < 2 * PAD, 1.0, 0.0)).astype(BF16)
    wanted = mm(picked, scale) - 1.0
    mem_copy.wait()
    piece = min(n * PAD, 256)
    for c in range(n * PAD // piece):
        hot = rowhot(wanted[c * piece:(c + 1) * piece], R)
        got = mm(hot, mem[...]).astype(BF16)
        served[pl.ds(c * piece // PAD, piece // PAD)] = got.reshape(piece // PAD, PAD, D)

    def serve(i, carry):
        to = plane(i)
        remote(served.at[to], rows.at[s], row_sem, (), to, r).start()
        return carry

    lax.fori_loop(1, n, serve, 0)
    rows[s] = served[s]

    src_row = src_ref[...].reshape(1, E).astype(F32)
    src_hot = rowhot(column(src_row), T)
    dst_hot = rowhot(column(dst_ref[...].reshape(1, E).astype(F32)), T)
    src_hot_t = one_hot(iota((T, E), 0).astype(F32) == src_row)
    slot_hot = rowhot(column(ownerf * float(PAD) + place), n * PAD)
    counts = mm(src_hot_t, jnp.ones((E, LANES), BF16))
    share = 1.0 / jnp.maximum(counts, 1.0)
    tick = tick_ref[...]
    tick_hi = column((tick >> 5).astype(F32)).astype(BF16)
    tick_lo = column((tick & 31).astype(F32)).astype(BF16)
    ticks = mm(src_hot, tick_hi) * 32.0 + mm(src_hot, tick_lo)
    spans = column(stamp_ref[...].reshape(1, E).astype(F32)) - ticks
    encode = jnp.cos(spans * freq_ref[...] + phase_ref[...]).astype(BF16)

    for i in range(1, m):
        finish(slots_all.at[0], slot_sem.at[1, i])
    rung = min(n * G, 384)

    def fill_place(c, carry):
        at = pl.multiple_of(c * rung, rung)
        line_no = (iota((rung, T), 0) + c * rung).astype(F32)
        for q in range(m):
            place_hot[pl.ds(at, rung), pl.ds(q * T, T)] = one_hot(line_no == slots_all[q])
        return carry

    lax.fori_loop(0, n * G // rung, fill_place, 0)

    for copy in own:
        copy.wait()

    def others(group, do):
        for i in range(1, m):
            for w, shard_ref, full, part, width in halves(group):
                cols = pl.ds(pl.multiple_of(line(i) * width, LANES), width)
                do(full.at[part, cols], w, i)

    def arrive(group):
        others(group, lambda ref, w, i: finish(ref, wx_sem.at[1, w, m - i]))
        others(group, lambda ref, w, i: remote(ref, ref, wc_sem, (w, i), sibling, r).start())

    arrive(groups[0])

    finish(rows.at[pl.ds(0, n - 1)], row_sem.at[1])
    fetched = mm(slot_hot, rows[...].reshape(n * PAD, D)).astype(BF16)
    hs[...] = mm(src_hot, fetched).astype(BF16)
    hd[...] = mm(dst_hot, fetched).astype(BF16)
    others(groups[0], lambda ref, w, i: finish(ref, wc_sem.at[1, w, i]))
    wide = 2 * LANES
    for c in range(D // wide):
        def gate(k):
            return slice(k * D + c * wide, k * D + (c + 1) * wide)
        reset = mm(hd[...], wi[:, gate(0)]) + mm(encode, wt[:, gate(0)]) + mm(hs[...], wh[:, gate(0)])
        update = mm(hd[...], wi[:, gate(1)]) + mm(encode, wt[:, gate(1)]) + mm(hs[...], wh[:, gate(1)])
        reset = 0.5 * jnp.tanh(0.5 * reset) + 0.5
        update = 0.5 * jnp.tanh(0.5 * update) + 0.5
        fresh = jnp.tanh(
            mm(hd[...], wi[:, gate(2)]) + mm(encode, wt[:, gate(2)]) + reset * mm(hs[...], wh[:, gate(2)])
        )
        hold = hs[:, c * wide:(c + 1) * wide].astype(F32)
        change = (1.0 - update) * (fresh - hold)
        hn[:, c * wide:(c + 1) * wide] = hold + change
        delta = mm(src_hot_t, change.astype(BF16))
        for k in range(2):
            dsend[2 * c + k] = (delta[:, k * LANES:(k + 1) * LANES] * share).astype(BF16)

    for i in range(1, m):
        remote(dsend.at[line(i)], dall.at[r], delta_sem, (i,), s, line(i)).start()
    dall[r] = dsend[r]
    for i in range(1, m):
        finish(dall.at[0], delta_sem.at[1, i])

    for c in range(n * G // rung):
        part = mm(place_hot[pl.ds(c * rung, rung)], dall[...].reshape(m * T, LANES)).astype(BF16)
        outbuf[pl.ds(c * rung // G, rung // G)] = part.reshape(rung // G, G, LANES)

    def post(i, carry):
        to = plane(i)
        remote(outbuf.at[to], landed.at[s], out_sem, (), to, r).start()
        return carry

    lax.fori_loop(1, n, post, 0)
    landed[s] = outbuf[s]

    for i in range(1, m):
        finish(asked_all.at[0], ask_sem.at[1, i])
    fan_no = jnp.floor((iota((n, n * G), 1).astype(F32) + 0.5) * (1.0 / G))
    fan = one_hot(fan_no == iota((n, n * G), 0).astype(F32))
    lane_no = iota((2 * PAD, n * G), 1).astype(F32)
    seat = lane_no - jnp.floor((lane_no + 0.5) * (1.0 / G)) * float(G)
    line_no = iota((2 * PAD, n * G), 0)
    weight = jnp.where(line_no < PAD, 32.0, 1.0)
    seat_of = (line_no & (PAD - 1)).astype(F32)
    target = jnp.full((1, n * G), -1.0, F32)
    for q in range(m):
        turned = jnp.transpose(asked_all[q])[:2 * PAD].astype(BF16)
        values = mm(turned, fan) * weight
        here = (seat == seat_of + float(q * cap)) & (seat_of < float(cap))
        target = target + jnp.sum(jnp.where(here, values, 0.0), axis=0, keepdims=True)
    step = LANES

    def fill_owner(c, carry):
        at = pl.multiple_of(c * step, step)
        owner_hot[pl.ds(at, step)] = one_hot((iota((step, n * G), 0) + c * step).astype(F32) == target)
        return carry

    lax.fori_loop(0, R // step, fill_owner, 0)

    arrive(groups[1])
    others(groups[1], lambda ref, w, i: finish(ref, wc_sem.at[1, w, i]))
    query = mm(hn[...].astype(BF16), wq[...]).astype(BF16)
    keyval = mm(hd[...], wk[...]).astype(BF16)
    head = D // H
    blocks = E // BLK
    block_no = iota((BLK, E), 1) >> 7
    for q in range(blocks):
        times = (block_no == listed_ref[0, q]).astype(F32) + (block_no == listed_ref[1, q]).astype(F32)
        seen = times > 0.0
        for h in range(H):
            cols = slice(h * head, (h + 1) * head)
            at = slice(q * BLK, (q + 1) * BLK)
            scores = mm_nt(query[at, cols], keyval[:, cols]) * (1.0 / math.sqrt(head))
            scores = jnp.where(seen, scores, -jnp.inf)
            top = jnp.max(scores, axis=1, keepdims=True)
            weighed = jnp.exp(scores - top) * times
            prob = (weighed / jnp.sum(weighed, axis=1, keepdims=True)).astype(BF16)
            attend = mm(prob, keyval[:, D + h * head:D + (h + 1) * head])
            embed_ref[at, cols] = (hn[at, cols] + attend).astype(BF16)

    finish(landed.at[pl.ds(0, n - 1)], out_sem.at[1])
    mycols = pl.ds(pl.multiple_of(r * LANES, LANES), LANES)
    step = min(R, 256)
    for c in range(R // step):
        total = mm(owner_hot[pl.ds(c * step, step)], landed[...].reshape(n * G, LANES))
        at = pl.ds(c * step, step)
        newcol[at] = (mem[at, mycols].astype(F32) + total).astype(BF16)
        for i in range(1, m):
            remote(newcol.at[at], new_ref.at[at, mycols], new_sem, (i,), s, line(i)).start()
    keep = pltpu.make_async_copy(newcol, new_ref.at[:, mycols], local_sem.at[0])
    keep.start()
    keep.wait()
    for i in range(1, m):
        finish(newcol, new_sem.at[1, i])

    finish(asked.at[pl.ds(0, n - 1)], req_sem.at[0])
    finish(rows.at[pl.ds(0, n - 1)], row_sem.at[0])
    finish(landed.at[pl.ds(0, n - 1)], out_sem.at[0])
    for i in range(1, m):
        finish(slots_all.at[0], slot_sem.at[0, i])
        finish(asked_all.at[0], ask_sem.at[0, i])
        finish(dall.at[0], delta_sem.at[0, i])
        finish(newcol, new_sem.at[0, i])
    for g in range(2):
        others(groups[g], lambda ref, w, i: finish(ref, wx_sem.at[0, w, i]))
        others(groups[g], lambda ref, w, i: finish(ref, wc_sem.at[0, w, i]))


def shards(
    memory, touch_owner, touch_row, touch_time, src_slot, dst_slot, event_time, neighbour_blocks,
    time_freq, time_phase, w_input, w_time, w_hidden, w_query, w_keyval,
):
    n = lax.axis_size("shard")
    m = lax.axis_size("rep")
    T = touch_row.shape[0]
    E = src_slot.shape[0]
    R, D = memory.shape
    cap = 2 * T // n + 2
    G = m * cap
    vmem = pl.BlockSpec(memory_space=pltpu.VMEM)
    anywhere = pl.BlockSpec(memory_space=pl.ANY)
    weights = (w_input, w_time, w_hidden, w_query, w_keyval)
    dma = pltpu.SemaphoreType.DMA
    return pl.pallas_call(
        functools.partial(body, n, m, cap),
        out_shape=(jax.ShapeDtypeStruct((E, D), BF16), jax.ShapeDtypeStruct((R, D), BF16)),
        in_specs=[vmem] * 6 + [pl.BlockSpec(memory_space=pltpu.SMEM)] + [vmem] * 2 + [anywhere] * 6,
        out_specs=(vmem, anywhere),
        scratch_shapes=[pltpu.VMEM((R, D), BF16)]
        + [pltpu.VMEM((w.shape[0], w.shape[1] * m), BF16) for w in weights]
        + [
            pltpu.VMEM((n, 1, LANES), F32),
            pltpu.VMEM((n, 1, LANES), F32),
            pltpu.VMEM((m, n, LANES), F32),
            pltpu.VMEM((m, 1, T), F32),
            pltpu.VMEM((n, PAD, D), BF16),
            pltpu.VMEM((n, PAD, D), BF16),
            pltpu.VMEM((n * G, m * T), BF16),
            pltpu.VMEM((R, n * G), BF16),
            pltpu.VMEM((E, D), BF16),
            pltpu.VMEM((E, D), BF16),
            pltpu.VMEM((E, D), F32),
            pltpu.VMEM((m, T, LANES), BF16),
            pltpu.VMEM((m, T, LANES), BF16),
            pltpu.VMEM((n, G, LANES), BF16),
            pltpu.VMEM((n, G, LANES), BF16),
            pltpu.VMEM((R, LANES), BF16),
            dma((6,)),
            dma((2,)),
            dma((2, m)),
            dma((2, m)),
            dma((2, len(weights), m)),
            dma((2, len(weights), m)),
            dma((2,)),
            dma((2, m)),
            dma((2,)),
            dma((2, m)),
        ],
        compiler_params=pltpu.CompilerParams(
            collective_id=0, has_side_effects=True, vmem_limit_bytes=56 * 1024 * 1024
        ),
    )(
        touch_owner.reshape(1, T), touch_row.reshape(1, T), touch_time.reshape(1, T),
        src_slot, dst_slot, event_time,
        neighbour_blocks.T, time_freq.reshape(1, -1), time_phase.reshape(1, -1),
        memory, *weights,
    )


def solution(mesh):
    both = P(("shard", "rep"))
    placed = (
        P("shard", None), P(("shard", "rep"), None), both, both, both, both, both,
        P(("shard", "rep"), None), P(), P(),
    ) + (P(None, "rep"),) * 5
    return jax.shard_map(
        shards,
        mesh=mesh,
        in_specs=placed,
        out_specs=(P(("shard", "rep"), None), P("shard", None)),
        check_vma=False,
    )
```

```python
import functools
import math

import jax
import jax.numpy as jnp
from jax import lax
from jax.experimental import pallas as pl
from jax.experimental.pallas import tpu as pltpu
from jax.sharding import PartitionSpec as P

H = 4
BLK = 128
LANES = 128
PAD = 8
YS = 8
CUTS = 8
F32 = jnp.float32
BF16 = jnp.bfloat16
I32 = jnp.int32


def mm(a, b):
    return jnp.dot(a, b, preferred_element_type=F32)


def mm_nt(a, b):
    return lax.dot_general(a, b, (((1,), (1,)), ((), ())), preferred_element_type=F32)


def mm_tn(a, b):
    return lax.dot_general(a, b, (((0,), (0,)), ((), ())), preferred_element_type=F32)


def iota(shape, dim):
    return lax.broadcasted_iota(I32, shape, dim)


def one_hot(cond):
    return jnp.where(cond, 1.0, 0.0).astype(BF16)


def column(row):
    return jnp.transpose(jnp.broadcast_to(row, (LANES, row.shape[1])))


def rowhot(col, width):
    lane = iota(col.shape, 1).astype(F32)
    parts = [one_hot(col == lane + float(k * LANES)) for k in range(pl.cdiv(width, LANES))]
    hot = parts[0] if len(parts) == 1 else jnp.concatenate(parts, axis=1)
    return hot if hot.shape[1] == width else hot[:, :width]


def body(
    n, m, cap,
    owner_ref, row_ref, tick_ref, src_ref, dst_ref, stamp_ref, listed_ref, freq_ref, phase_ref,
    mem_hbm, wi_hbm, wt_hbm, wh_hbm, wq_hbm, wk_hbm,
    embed_ref, new_ref,
    mem, wi, wt, wh, wq, wk,
    reqbuf, halfway, asked, asked_all, slots_all, served, rows, place_hot, owner_hot,
    hs, hd, hn, dsend, dall, outbuf, landed, newcol, want, slot_hot, total,
    local_sem, req_sem, slot_sem, ask_sem, wx_sem, wc_sem, row_sem, delta_sem, out_sem, new_sem,
):
    s = lax.axis_index("shard")
    r = lax.axis_index("rep")
    T = owner_ref.shape[1]
    E = src_ref.shape[0]
    R, D = mem.shape
    G = m * cap
    W = n // YS
    core = lax.rem(s, 2)
    sibling = s + 1 - 2 * core

    def line(i):
        return lax.rem(r + i, m)

    def remote(src, dst, sems, at, shard, rep):
        return pltpu.make_async_remote_copy(
            src_ref=src, dst_ref=dst, send_sem=sems.at[(0,) + at], recv_sem=sems.at[(1,) + at],
            device_id=(shard, rep), device_id_type=pl.DeviceIdType.MESH,
        )

    def finish(ref, sem):
        pltpu.make_async_copy(ref, ref, sem).wait()

    weights = ((wi_hbm, wi), (wt_hbm, wt), (wh_hbm, wh), (wq_hbm, wq), (wk_hbm, wk))
    mem_copy = pltpu.make_async_copy(mem_hbm, mem, local_sem.at[0])
    mem_copy.start()
    own = []
    for at, (shard_ref, full) in enumerate(weights):
        width = shard_ref.shape[1]
        copy = pltpu.make_async_copy(
            shard_ref, full.at[:, pl.ds(pl.multiple_of(r * width, LANES), width)], local_sem.at[1 + at]
        )
        copy.start()
        own.append(copy)

    barrier = pltpu.get_barrier_semaphore()

    yy = s // W
    ww = lax.rem(s, W)

    def signal(sem, shard, rep):
        pl.semaphore_signal(sem, inc=1, device_id=(shard, rep), device_id_type=pl.DeviceIdType.MESH)

    for i in range(1, YS):
        signal(barrier, lax.rem(yy + i, YS) * W + ww, r)

    def greet(i, carry):
        signal(barrier, yy * W + lax.rem(ww + i, W), r)
        return carry

    lax.fori_loop(1, W, greet, 0)
    for i in range(1, m):
        signal(barrier, s, line(i))
    rows[...] = jnp.zeros_like(rows)

    half = YS // 2
    turns = (2, 1, 3, 0)

    def quarter(turn):
        return lax.rem(yy // 2 + turn, half)

    def scatter(lines, send):
        def pick(q, carry):
            for k, (turn, which) in enumerate(lines):
                at = lax.rem(ww + q * 5 + k * 3 + W // 2, W)
                to = (quarter(turn) * 2 + which) * W + at
                if turn:
                    send(turn, to)
                else:
                    pl.when(to != s)(lambda: send(turn, to))
            return carry

        lax.fori_loop(0, W, pick, 0)

    first_lines = ((2, 0), (2, 1))
    other_lines = ((1, 1), (3, 0), (1, 0), (3, 1), (0, 0), (0, 1))

    def group_size(turn):
        return 2 * W if turn else 2 * W - 1

    owner = owner_ref[...]
    hit = one_hot(iota((n, T), 0) == owner)
    earlier = one_hot(iota((T, T), 0) < iota((T, T), 1))
    place = jnp.sum(mm(hit, earlier) * hit.astype(F32), axis=0, keepdims=True)
    asked_row = row_ref[...] + 1
    line_at = iota((LANES, T), 0).astype(F32)
    ask_hi = (asked_row >> 5).astype(F32)
    ask_lo = (asked_row & 31).astype(F32)
    table = jnp.where(line_at == place, ask_hi, jnp.where(line_at == place + float(PAD), ask_lo, 0.0))
    reqbuf[...] = mm_nt(hit, table.astype(BF16)).reshape(YS, W, 1, LANES)
    ownerf = owner.astype(F32)
    slots_all[r] = ownerf * float(G) + place + (r * cap).astype(F32)
    halfway[yy] = reqbuf[yy]

    pl.semaphore_wait(barrier, YS - 1 + W - 1 + m - 1)

    for i in range(1, YS):
        y = lax.rem(yy + i, YS)
        remote(reqbuf.at[y], halfway.at[yy], req_sem, (0,), y * W + ww, r).start()
    finish(halfway.at[pl.ds(0, YS - 1)], req_sem.at[1, 0])

    def ask(i, carry):
        w = lax.rem(ww + i, W)
        remote(halfway.at[:, w], asked.at[:, ww], req_sem, (1,), yy * W + w, r).start()
        return carry

    lax.fori_loop(1, W, ask, 0)
    asked[:, ww] = halfway[:, ww]
    for i in range(1, m):
        remote(slots_all.at[r], slots_all.at[r], slot_sem, (i,), s, line(i)).start()

    def halves(group):
        out = []
        for w in group:
            shard_ref, full = weights[w]
            depth, width = shard_ref.shape
            half = depth // 2
            out.append((w, shard_ref, full, pl.ds(pl.multiple_of(core * half, PAD), half), width))
        return out

    groups = ((1, 2, 0), (3, 4))

    def give(group):
        for i in range(1, m):
            for w, shard_ref, full, part, width in halves(group):
                cols = pl.ds(pl.multiple_of(r * width, LANES), width)
                remote(shard_ref.at[part], full.at[part, cols], wx_sem, (w, i), s, line(i)).start()

    give(groups[0])

    finish(asked.at[:, pl.ds(0, W - 1)], req_sem.at[1, 1])
    table_in = asked[...].reshape(n, LANES)
    asked_all[r] = table_in
    for i in range(1, m):
        remote(asked_all.at[r], asked_all.at[r], ask_sem, (i,), s, line(i)).start()
    spread = one_hot((iota((n * PAD, n), 0) >> 3) == iota((n * PAD, n), 1))
    lane = iota((n * PAD, LANES), 1)
    mine = ((lane & (PAD - 1)) == (iota((n * PAD, LANES), 0) & (PAD - 1))) & (lane < 2 * PAD)
    picked = jnp.where(mine, mm(spread, table_in.astype(BF16)), 0.0).astype(BF16)
    depth_at = iota((LANES, LANES), 0)
    scale = jnp.where(depth_at < PAD, 32.0, jnp.where(depth_at < 2 * PAD, 1.0, 0.0)).astype(BF16)
    want[...] = mm(picked, scale) - 1.0
    mem_copy.wait()
    piece = 2 * W * PAD

    def serve(turn, to):
        remote(served.at[to, pl.ds(0, cap)], rows.at[s, pl.ds(0, cap)], row_sem, (turn,), to, r).start()

    for turn in turns:
        first = quarter(turn) * 2 * W
        hot = rowhot(want[pl.ds(pl.multiple_of(first * PAD, piece), piece)], R)
        served[pl.ds(first, 2 * W)] = mm(hot, mem[...]).astype(BF16).reshape(2 * W, PAD, D)
        if turn == turns[0]:
            scatter(first_lines, serve)
    scatter(other_lines, serve)
    rows[s] = served[s]

    src_row = src_ref[...].reshape(1, E).astype(F32)
    src_hot = rowhot(column(src_row), T)
    dst_hot = rowhot(column(dst_ref[...].reshape(1, E).astype(F32)), T)
    src_hot_t = one_hot(iota((T, E), 0).astype(F32) == src_row)
    slot_hot[...] = rowhot(column(ownerf * float(PAD) + place), n * PAD)
    counts = mm(src_hot_t, jnp.ones((E, LANES), BF16))
    share = 1.0 / jnp.maximum(counts, 1.0)
    tick = tick_ref[...]
    tick_hi = column((tick >> 5).astype(F32)).astype(BF16)
    tick_lo = column((tick & 31).astype(F32)).astype(BF16)
    ticks = mm(src_hot, tick_hi) * 32.0 + mm(src_hot, tick_lo)
    spans = column(stamp_ref[...].reshape(1, E).astype(F32)) - ticks
    encode = jnp.cos(spans * freq_ref[...] + phase_ref[...]).astype(BF16)

    for i in range(1, m):
        finish(slots_all.at[0], slot_sem.at[1, i])
    rung = min(n * G, 384)

    def fill_place(c, carry):
        at = pl.multiple_of(c * rung, rung)
        line_no = (iota((rung, T), 0) + c * rung).astype(F32)
        for q in range(m):
            place_hot[pl.ds(at, rung), pl.ds(q * T, T)] = one_hot(line_no == slots_all[q])
        return carry

    lax.fori_loop(0, n * G // rung, fill_place, 0)

    for copy in own:
        copy.wait()

    def others(group, do):
        for i in range(1, m):
            for w, shard_ref, full, part, width in halves(group):
                cols = pl.ds(pl.multiple_of(line(i) * width, LANES), width)
                do(full.at[part, cols], w, i)

    def arrive(group):
        others(group, lambda ref, w, i: finish(ref, wx_sem.at[1, w, m - i]))
        others(group, lambda ref, w, i: remote(ref, ref, wc_sem, (w, i), sibling, r).start())

    arrive(groups[0])

    fetched = jnp.zeros((T, D), F32)
    for turn in turns:
        finish(rows.at[pl.ds(0, group_size(turn)), pl.ds(0, cap)], row_sem.at[1, turn])
        first = quarter(half - turn) * 2 * W
        came = slot_hot[:, pl.ds(pl.multiple_of(first * PAD, piece), piece)]
        fetched = fetched + mm(came, rows[pl.ds(first, 2 * W)].reshape(piece, D))
    fetched = fetched.astype(BF16)
    hs[...] = mm(src_hot, fetched).astype(BF16)
    hd[...] = mm(dst_hot, fetched).astype(BF16)
    others(groups[0], lambda ref, w, i: finish(ref, wc_sem.at[1, w, i]))
    wide = 2 * LANES

    def delta_copy(to):
        return pltpu.make_async_remote_copy(
            src_ref=dsend.at[to], dst_ref=dall.at[r], send_sem=delta_sem.at[0, to], recv_sem=delta_sem.at[1, r],
            device_id=(s, to), device_id_type=pl.DeviceIdType.MESH,
        )

    for c in range(D // wide):
        def gate(k):
            return slice(k * D + c * wide, k * D + (c + 1) * wide)
        reset = mm(hd[...], wi[:, gate(0)]) + mm(encode, wt[:, gate(0)]) + mm(hs[...], wh[:, gate(0)])
        update = mm(hd[...], wi[:, gate(1)]) + mm(encode, wt[:, gate(1)]) + mm(hs[...], wh[:, gate(1)])
        reset = 0.5 * jnp.tanh(0.5 * reset) + 0.5
        update = 0.5 * jnp.tanh(0.5 * update) + 0.5
        fresh = jnp.tanh(
            mm(hd[...], wi[:, gate(2)]) + mm(encode, wt[:, gate(2)]) + reset * mm(hs[...], wh[:, gate(2)])
        )
        hold = hs[:, c * wide:(c + 1) * wide].astype(F32)
        change = (1.0 - update) * (fresh - hold)
        hn[:, c * wide:(c + 1) * wide] = hold + change
        delta = mm(src_hot_t, change.astype(BF16))
        for k in range(2):
            to = 2 * c + k
            dsend[to] = (delta[:, k * LANES:(k + 1) * LANES] * share).astype(BF16)

            @pl.when(r != to)
            def _():
                delta_copy(to).start()

    dall[r] = dsend[r]
    for i in range(1, m):
        finish(dall.at[0], delta_sem.at[1, line(i)])
    give(groups[1])

    def post(turn, to):
        remote(outbuf.at[to], landed.at[s], out_sem, (turn,), to, r).start()

    span = 2 * W * G
    for turn in turns:
        first = quarter(turn) * 2 * W
        part = mm(place_hot[pl.ds(pl.multiple_of(first * G, span), span)], dall[...].reshape(m * T, LANES))
        outbuf[pl.ds(first, 2 * W)] = part.astype(BF16).reshape(2 * W, G, LANES)
        if turn == turns[0]:
            scatter(first_lines, post)
    scatter(other_lines, post)
    landed[s] = outbuf[s]

    for i in range(1, m):
        finish(asked_all.at[0], ask_sem.at[1, i])
    fan_no = jnp.floor((iota((n, n * G), 1).astype(F32) + 0.5) * (1.0 / G))
    fan = one_hot(fan_no == iota((n, n * G), 0).astype(F32))
    lane_no = iota((2 * PAD, n * G), 1).astype(F32)
    seat = lane_no - jnp.floor((lane_no + 0.5) * (1.0 / G)) * float(G)
    line_no = iota((2 * PAD, n * G), 0)
    weight = jnp.where(line_no < PAD, 32.0, 1.0)
    seat_of = (line_no & (PAD - 1)).astype(F32)
    target = jnp.full((1, n * G), -1.0, F32)
    for q in range(m):
        turned = jnp.transpose(asked_all[q])[:2 * PAD].astype(BF16)
        values = mm(turned, fan) * weight
        here = (seat == seat_of + float(q * cap)) & (seat_of < float(cap))
        target = target + jnp.sum(jnp.where(here, values, 0.0), axis=0, keepdims=True)
    step = LANES

    def fill_owner(c, carry):
        at = pl.multiple_of(c * step, step)
        owner_hot[pl.ds(at, step)] = one_hot((iota((step, n * G), 0) + c * step).astype(F32) == target)
        return carry

    lax.fori_loop(0, R // step, fill_owner, 0)

    arrive(groups[1])
    others(groups[1], lambda ref, w, i: finish(ref, wc_sem.at[1, w, i]))
    query = mm(hn[...].astype(BF16), wq[...]).astype(BF16)
    keyval = mm(hd[...], wk[...]).astype(BF16)
    head = D // H
    blocks = E // BLK
    block_no = iota((BLK, E), 1) >> 7
    for q in range(blocks):
        times = (block_no == listed_ref[0, q]).astype(F32) + (block_no == listed_ref[1, q]).astype(F32)
        seen = times > 0.0
        for h in range(H):
            cols = slice(h * head, (h + 1) * head)
            at = slice(q * BLK, (q + 1) * BLK)
            scores = mm_nt(query[at, cols], keyval[:, cols]) * (1.0 / math.sqrt(head))
            scores = jnp.where(seen, scores, -jnp.inf)
            top = jnp.max(scores, axis=1, keepdims=True)
            weighed = jnp.exp(scores - top) * times
            prob = (weighed / jnp.sum(weighed, axis=1, keepdims=True)).astype(BF16)
            attend = mm(prob, keyval[:, D + h * head:D + (h + 1) * head])
            embed_ref[at, cols] = (hn[at, cols] + attend).astype(BF16)

    def cols_of(rep):
        return pl.ds(pl.multiple_of(rep * LANES, LANES), LANES)

    def landed_part(turn, lines):
        first = quarter(half - turn) * 2 * W
        hot = owner_hot[lines, pl.ds(pl.multiple_of(first * G, span), span)]
        return mm(hot, landed[pl.ds(first, 2 * W)].reshape(span, LANES))

    right, left = line(1), line(m - 1)
    for turn in turns[:-1]:
        finish(landed.at[pl.ds(0, group_size(turn))], out_sem.at[1, turn])
        part = landed_part(turn, slice(None))
        total[...] = part if turn == turns[0] else total[...] + part
    turn = turns[-1]
    finish(landed.at[pl.ds(0, group_size(turn))], out_sem.at[1, turn])
    step = R // CUTS

    def new_copy(kind, c, src, owner_rep, to):
        at = (pl.ds(c * step, step), cols_of(owner_rep))
        return remote(new_ref.at[at] if src is None else src, new_ref.at[at], new_sem, (kind, c), s, to)

    for c in range(CUTS):
        at = pl.ds(c * step, step)
        newcol[at] = (mem[at, cols_of(r)].astype(F32) + (total[at] + landed_part(turn, at))).astype(BF16)
        new_copy(0, c, newcol.at[at], r, right).start()
        new_copy(1, c, newcol.at[at], r, left).start()
    keep = pltpu.make_async_copy(newcol, new_ref.at[:, cols_of(r)], local_sem.at[0])
    keep.start()
    for c in range(CUTS):
        if c % 2 == 0:
            finish(newcol.at[pl.ds(0, step)], new_sem.at[1, 0, c])
            new_copy(2, c, None, left, right).start()
        else:
            finish(newcol.at[pl.ds(0, step)], new_sem.at[1, 1, c])
            new_copy(3, c, None, right, left).start()
    keep.wait()
    for c in range(CUTS):
        finish(newcol.at[pl.ds(0, step)], new_sem.at[1, 1 - c % 2, c])
        finish(newcol.at[pl.ds(0, step)], new_sem.at[1, 2 + c % 2, c])

    finish(halfway.at[pl.ds(0, YS - 1)], req_sem.at[0, 0])
    finish(asked.at[:, pl.ds(0, W - 1)], req_sem.at[0, 1])
    for turn in turns:
        finish(rows.at[pl.ds(0, group_size(turn)), pl.ds(0, cap)], row_sem.at[0, turn])
        finish(landed.at[pl.ds(0, group_size(turn))], out_sem.at[0, turn])
    for c in range(CUTS):
        for kind in (0, 1, 2 + c % 2):
            finish(newcol.at[pl.ds(0, step)], new_sem.at[0, kind, c])
    for i in range(1, m):
        finish(slots_all.at[0], slot_sem.at[0, i])
        finish(asked_all.at[0], ask_sem.at[0, i])
        finish(dall.at[0], delta_sem.at[0, line(i)])
    for g in range(2):
        others(groups[g], lambda ref, w, i: finish(ref, wx_sem.at[0, w, i]))
        others(groups[g], lambda ref, w, i: finish(ref, wc_sem.at[0, w, i]))


def settle(embed_in, new_in, embed_out, new_out, embed_buf, new_buf, sems):
    moves = []
    for src, buf, dst, count in ((new_in, new_buf, new_out, 4), (embed_in, embed_buf, embed_out, 2)):
        size = src.shape[0] // count
        for c in range(count):
            at = pl.ds(c * size, size)
            k = len(moves)
            moves.append((
                pltpu.make_async_copy(src.at[at], buf.at[at], sems.at[0, k]),
                pltpu.make_async_copy(buf.at[at], dst.at[at], sems.at[1, k]),
            ))
            moves[-1][0].start()
    for come, go in moves:
        come.wait()
        go.start()
    for come, go in moves:
        go.wait()


def shards(
    memory, touch_owner, touch_row, touch_time, src_slot, dst_slot, event_time, neighbour_blocks,
    time_freq, time_phase, w_input, w_time, w_hidden, w_query, w_keyval,
):
    n = lax.axis_size("shard")
    m = lax.axis_size("rep")
    T = touch_row.shape[0]
    E = src_slot.shape[0]
    R, D = memory.shape
    cap = 2 * T // n + 2
    G = m * cap
    vmem = pl.BlockSpec(memory_space=pltpu.VMEM)
    anywhere = pl.BlockSpec(memory_space=pl.ANY)
    weights = (w_input, w_time, w_hidden, w_query, w_keyval)
    dma = pltpu.SemaphoreType.DMA
    embed, new_memory = pl.pallas_call(
        functools.partial(body, n, m, cap),
        out_shape=(jax.ShapeDtypeStruct((E, D), BF16), jax.ShapeDtypeStruct((R, D), BF16)),
        in_specs=[vmem] * 6 + [pl.BlockSpec(memory_space=pltpu.SMEM)] + [vmem] * 2 + [anywhere] * 6,
        out_specs=(vmem, anywhere),
        scratch_shapes=[pltpu.VMEM((R, D), BF16)]
        + [pltpu.VMEM((w.shape[0], w.shape[1] * m), BF16) for w in weights]
        + [
            pltpu.VMEM((YS, n // YS, 1, LANES), F32),
            pltpu.VMEM((YS, n // YS, 1, LANES), F32),
            pltpu.VMEM((YS, n // YS, 1, LANES), F32),
            pltpu.VMEM((m, n, LANES), F32),
            pltpu.VMEM((m, 1, T), F32),
            pltpu.VMEM((n, PAD, D), BF16),
            pltpu.VMEM((n, PAD, D), BF16),
            pltpu.VMEM((n * G, m * T), BF16),
            pltpu.VMEM((R, n * G), BF16),
            pltpu.VMEM((E, D), BF16),
            pltpu.VMEM((E, D), BF16),
            pltpu.VMEM((E, D), F32),
            pltpu.VMEM((m, T, LANES), BF16),
            pltpu.VMEM((m, T, LANES), BF16),
            pltpu.VMEM((n, G, LANES), BF16),
            pltpu.VMEM((n, G, LANES), BF16),
            pltpu.VMEM((R, LANES), BF16),
            pltpu.VMEM((n * PAD, LANES), F32),
            pltpu.VMEM((T, n * PAD), BF16),
            pltpu.VMEM((R, LANES), F32),
            dma((6,)),
            dma((2, 2)),
            dma((2, m)),
            dma((2, m)),
            dma((2, len(weights), m)),
            dma((2, len(weights), m)),
            dma((2, YS // 2)),
            dma((2, m)),
            dma((2, YS // 2)),
            dma((2, 4, CUTS)),
        ],
        compiler_params=pltpu.CompilerParams(
            collective_id=0, has_side_effects=True, vmem_limit_bytes=56 * 1024 * 1024
        ),
    )(
        touch_owner.reshape(1, T), touch_row.reshape(1, T), touch_time.reshape(1, T),
        src_slot, dst_slot, event_time,
        neighbour_blocks.T, time_freq.reshape(1, -1), time_phase.reshape(1, -1),
        memory, *weights,
    )
    return pl.pallas_call(
        settle,
        out_shape=(jax.ShapeDtypeStruct((E, D), BF16), jax.ShapeDtypeStruct((R, D), BF16)),
        in_specs=[anywhere] * 2,
        out_specs=(anywhere, anywhere),
        scratch_shapes=[pltpu.VMEM((E, D), BF16), pltpu.VMEM((R, D), BF16), dma((2, 6))],
        cost_estimate=pl.CostEstimate(flops=0, bytes_accessed=4 * (E + R) * D, transcendentals=0),
    )(embed, new_memory)


def solution(mesh):
    both = P(("shard", "rep"))
    placed = (
        P("shard", None), P(("shard", "rep"), None), both, both, both, both, both,
        P(("shard", "rep"), None), P(), P(),
    ) + (P(None, "rep"),) * 5
    return jax.shard_map(
        shards,
        mesh=mesh,
        in_specs=placed,
        out_specs=(P(("shard", "rep"), None), P("shard", None)),
        check_vma=False,
    )
```

```python
import functools
import math

import jax
import jax.numpy as jnp
from jax import lax
from jax.experimental import pallas as pl
from jax.experimental.pallas import tpu as pltpu
from jax.sharding import PartitionSpec as P

H = 4
BLK = 128
LANES = 128
PAD = 8
YS = 8
CUTS = 8
F32 = jnp.float32
BF16 = jnp.bfloat16
I32 = jnp.int32


def mm(a, b):
    return jnp.dot(a, b, preferred_element_type=F32)


def mm_nt(a, b):
    return lax.dot_general(a, b, (((1,), (1,)), ((), ())), preferred_element_type=F32)


def mm_tn(a, b):
    return lax.dot_general(a, b, (((0,), (0,)), ((), ())), preferred_element_type=F32)


def iota(shape, dim):
    return lax.broadcasted_iota(I32, shape, dim)


def one_hot(cond):
    return jnp.where(cond, 1.0, 0.0).astype(BF16)


def column(row):
    return jnp.transpose(jnp.broadcast_to(row, (LANES, row.shape[1])))


def rowhot(col, width):
    lane = iota(col.shape, 1).astype(F32)
    parts = [one_hot(col == lane + float(k * LANES)) for k in range(pl.cdiv(width, LANES))]
    hot = parts[0] if len(parts) == 1 else jnp.concatenate(parts, axis=1)
    return hot if hot.shape[1] == width else hot[:, :width]


def body(
    n, m, cap,
    *refs,
):
    small_hbm, refs = refs[:9], refs[9:]
    (
        mem_hbm, wi_hbm, wt_hbm, wh_hbm, wq_hbm, wk_hbm, embed_hbm, new_ref,
    ), refs = refs[:8], refs[8:]
    small, small_sem, embed_ref, refs = refs[:9], refs[9], refs[10], refs[11:]
    owner_ref, row_ref, tick_ref, src_ref, dst_ref, stamp_ref, listed_ref, freq_ref, phase_ref = small
    (
    mem, wi, wt, wh, wq, wk,
    reqbuf, halfway, asked, asked_all, slots_all, served, rows, place_hot, owner_hot,
    hs, hd, hn, dsend, dall, outbuf, landed, newcol, want, slot_hot, total,
    local_sem, req_sem, slot_sem, ask_sem, wx_sem, wc_sem, row_sem, delta_sem, out_sem, new_sem,
    ) = refs
    s = lax.axis_index("shard")
    r = lax.axis_index("rep")
    T = owner_ref.shape[1]
    E = src_ref.shape[0]
    R, D = mem.shape
    G = m * cap
    W = n // YS
    core = lax.rem(s, 2)
    sibling = s + 1 - 2 * core

    def line(i):
        return lax.rem(r + i, m)

    def remote(src, dst, sems, at, shard, rep):
        return pltpu.make_async_remote_copy(
            src_ref=src, dst_ref=dst, send_sem=sems.at[(0,) + at], recv_sem=sems.at[(1,) + at],
            device_id=(shard, rep), device_id_type=pl.DeviceIdType.MESH,
        )

    def finish(ref, sem):
        pltpu.make_async_copy(ref, ref, sem).wait()

    small_copies = [
        pltpu.make_async_copy(src, dst, small_sem.at[k]) for k, (src, dst) in enumerate(zip(small_hbm, small))
    ]
    for copy in small_copies:
        copy.start()
    weights = ((wi_hbm, wi), (wt_hbm, wt), (wh_hbm, wh), (wq_hbm, wq), (wk_hbm, wk))
    mem_copy = pltpu.make_async_copy(mem_hbm, mem, local_sem.at[0])
    mem_copy.start()
    own = []
    for at, (shard_ref, full) in enumerate(weights):
        width = shard_ref.shape[1]
        copy = pltpu.make_async_copy(
            shard_ref, full.at[:, pl.ds(pl.multiple_of(r * width, LANES), width)], local_sem.at[1 + at]
        )
        copy.start()
        own.append(copy)

    barrier = pltpu.get_barrier_semaphore()

    yy = s // W
    ww = lax.rem(s, W)

    def signal(sem, shard, rep):
        pl.semaphore_signal(sem, inc=1, device_id=(shard, rep), device_id_type=pl.DeviceIdType.MESH)

    for i in range(1, YS):
        signal(barrier, lax.rem(yy + i, YS) * W + ww, r)

    def greet(i, carry):
        signal(barrier, yy * W + lax.rem(ww + i, W), r)
        return carry

    lax.fori_loop(1, W, greet, 0)
    for i in range(1, m):
        signal(barrier, s, line(i))
    rows[...] = jnp.zeros_like(rows)

    half = YS // 2
    turns = (2, 1, 3, 0)

    def quarter(turn):
        return lax.rem(yy // 2 + turn, half)

    def scatter(lines, send):
        def pick(q, carry):
            for k, (turn, which) in enumerate(lines):
                at = lax.rem(ww + q * 5 + k * 3 + W // 2, W)
                to = (quarter(turn) * 2 + which) * W + at
                if turn:
                    send(turn, to)
                else:
                    pl.when(to != s)(lambda: send(turn, to))
            return carry

        lax.fori_loop(0, W, pick, 0)

    first_lines = ((2, 0), (2, 1))
    other_lines = ((1, 1), (3, 0), (1, 0), (3, 1), (0, 0), (0, 1))

    def group_size(turn):
        return 2 * W if turn else 2 * W - 1

    for copy in small_copies[:2]:
        copy.wait()
    owner = owner_ref[...]
    hit = one_hot(iota((n, T), 0) == owner)
    earlier = one_hot(iota((T, T), 0) < iota((T, T), 1))
    place = jnp.sum(mm(hit, earlier) * hit.astype(F32), axis=0, keepdims=True)
    asked_row = row_ref[...] + 1
    line_at = iota((LANES, T), 0).astype(F32)
    ask_hi = (asked_row >> 5).astype(F32)
    ask_lo = (asked_row & 31).astype(F32)
    table = jnp.where(line_at == place, ask_hi, jnp.where(line_at == place + float(PAD), ask_lo, 0.0))
    reqbuf[...] = mm_nt(hit, table.astype(BF16)).reshape(YS, W, 1, LANES)
    ownerf = owner.astype(F32)
    slots_all[r] = ownerf * float(G) + place + (r * cap).astype(F32)
    halfway[yy] = reqbuf[yy]

    pl.semaphore_wait(barrier, YS - 1 + W - 1 + m - 1)

    for i in range(1, YS):
        y = lax.rem(yy + i, YS)
        remote(reqbuf.at[y], halfway.at[yy], req_sem, (0,), y * W + ww, r).start()
    finish(halfway.at[pl.ds(0, YS - 1)], req_sem.at[1, 0])

    def ask(i, carry):
        w = lax.rem(ww + i, W)
        remote(halfway.at[:, w], asked.at[:, ww], req_sem, (1,), yy * W + w, r).start()
        return carry

    lax.fori_loop(1, W, ask, 0)
    asked[:, ww] = halfway[:, ww]
    for i in range(1, m):
        remote(slots_all.at[r], slots_all.at[r], slot_sem, (i,), s, line(i)).start()

    def halves(group):
        out = []
        for w in group:
            shard_ref, full = weights[w]
            depth, width = shard_ref.shape
            half = depth // 2
            out.append((w, shard_ref, full, pl.ds(pl.multiple_of(core * half, PAD), half), width))
        return out

    groups = ((1, 2, 0), (3, 4))

    def give(group):
        for i in range(1, m):
            for w, shard_ref, full, part, width in halves(group):
                cols = pl.ds(pl.multiple_of(r * width, LANES), width)
                remote(shard_ref.at[part], full.at[part, cols], wx_sem, (w, i), s, line(i)).start()

    give(groups[0])

    finish(asked.at[:, pl.ds(0, W - 1)], req_sem.at[1, 1])
    table_in = asked[...].reshape(n, LANES)
    spread = one_hot((iota((n * PAD, n), 0) >> 3) == iota((n * PAD, n), 1))
    lane = iota((n * PAD, LANES), 1)
    mine = ((lane & (PAD - 1)) == (iota((n * PAD, LANES), 0) & (PAD - 1))) & (lane < 2 * PAD)
    picked = jnp.where(mine, mm(spread, table_in.astype(BF16)), 0.0).astype(BF16)
    depth_at = iota((LANES, LANES), 0)
    scale = jnp.where(depth_at < PAD, 32.0, jnp.where(depth_at < 2 * PAD, 1.0, 0.0)).astype(BF16)
    want[...] = mm(picked, scale) - 1.0
    mem_copy.wait()
    piece = 2 * W * PAD

    def serve(turn, to):
        remote(served.at[to, pl.ds(0, cap)], rows.at[s, pl.ds(0, cap)], row_sem, (turn,), to, r).start()

    for turn in turns:
        first = quarter(turn) * 2 * W
        hot = rowhot(want[pl.ds(pl.multiple_of(first * PAD, piece), piece)], R)
        served[pl.ds(first, 2 * W)] = mm(hot, mem[...]).astype(BF16).reshape(2 * W, PAD, D)
        if turn == turns[0]:
            scatter(first_lines, serve)
    scatter(other_lines, serve)
    rows[s] = served[s]
    asked_all[r] = table_in
    for i in range(1, m):
        remote(asked_all.at[r], asked_all.at[r], ask_sem, (i,), s, line(i)).start()

    for copy in small_copies[2:]:
        copy.wait()
    src_row = src_ref[...].reshape(1, E).astype(F32)
    src_hot = rowhot(column(src_row), T)
    dst_hot = rowhot(column(dst_ref[...].reshape(1, E).astype(F32)), T)
    src_hot_t = one_hot(iota((T, E), 0).astype(F32) == src_row)
    slot_hot[...] = rowhot(column(ownerf * float(PAD) + place), n * PAD)
    counts = mm(src_hot_t, jnp.ones((E, LANES), BF16))
    share = 1.0 / jnp.maximum(counts, 1.0)
    tick = tick_ref[...]
    tick_hi = column((tick >> 5).astype(F32)).astype(BF16)
    tick_lo = column((tick & 31).astype(F32)).astype(BF16)
    ticks = mm(src_hot, tick_hi) * 32.0 + mm(src_hot, tick_lo)
    spans = column(stamp_ref[...].reshape(1, E).astype(F32)) - ticks
    encode = jnp.cos(spans * freq_ref[...] + phase_ref[...]).astype(BF16)

    for i in range(1, m):
        finish(slots_all.at[0], slot_sem.at[1, i])
    rung = min(n * G, 384)

    def fill_place(c, carry):
        at = pl.multiple_of(c * rung, rung)
        line_no = (iota((rung, T), 0) + c * rung).astype(F32)
        for q in range(m):
            place_hot[pl.ds(at, rung), pl.ds(q * T, T)] = one_hot(line_no == slots_all[q])
        return carry

    lax.fori_loop(0, n * G // rung, fill_place, 0)

    for copy in own:
        copy.wait()

    def others(group, do):
        for i in range(1, m):
            for w, shard_ref, full, part, width in halves(group):
                cols = pl.ds(pl.multiple_of(line(i) * width, LANES), width)
                do(full.at[part, cols], w, i)

    def arrive(group):
        others(group, lambda ref, w, i: finish(ref, wx_sem.at[1, w, m - i]))
        others(group, lambda ref, w, i: remote(ref, ref, wc_sem, (w, i), sibling, r).start())

    arrive(groups[0])

    fetched = jnp.zeros((T, D), F32)
    for turn in turns:
        finish(rows.at[pl.ds(0, group_size(turn)), pl.ds(0, cap)], row_sem.at[1, turn])
        first = quarter(half - turn) * 2 * W
        came = slot_hot[:, pl.ds(pl.multiple_of(first * PAD, piece), piece)]
        fetched = fetched + mm(came, rows[pl.ds(first, 2 * W)].reshape(piece, D))
    fetched = fetched.astype(BF16)
    hs[...] = mm(src_hot, fetched).astype(BF16)
    hd[...] = mm(dst_hot, fetched).astype(BF16)
    others(groups[0], lambda ref, w, i: finish(ref, wc_sem.at[1, w, i]))
    wide = 2 * LANES
    sent = []

    def delta_copy(to):
        return pltpu.make_async_remote_copy(
            src_ref=dsend.at[to], dst_ref=dall.at[r], send_sem=delta_sem.at[0, to], recv_sem=delta_sem.at[1, r],
            device_id=(s, to), device_id_type=pl.DeviceIdType.MESH,
        )

    for c in (1 - r // 2, r // 2):
        here = pl.ds(pl.multiple_of(c * wide, wide), wide)

        def gate(k):
            return pl.ds(pl.multiple_of(k * D + c * wide, wide), wide)

        reset = mm(hd[...], wi[:, gate(0)]) + mm(encode, wt[:, gate(0)]) + mm(hs[...], wh[:, gate(0)])
        update = mm(hd[...], wi[:, gate(1)]) + mm(encode, wt[:, gate(1)]) + mm(hs[...], wh[:, gate(1)])
        reset = 0.5 * jnp.tanh(0.5 * reset) + 0.5
        update = 0.5 * jnp.tanh(0.5 * update) + 0.5
        fresh = jnp.tanh(
            mm(hd[...], wi[:, gate(2)]) + mm(encode, wt[:, gate(2)]) + reset * mm(hs[...], wh[:, gate(2)])
        )
        hold = hs[:, here].astype(F32)
        change = (1.0 - update) * (fresh - hold)
        hn[:, here] = hold + change
        delta = mm(src_hot_t, change.astype(BF16))
        for k in range(2):
            dsend[2 * c + k] = (delta[:, k * LANES:(k + 1) * LANES] * share).astype(BF16)
        if not sent:
            delta_copy(line(2)).start()
            delta_copy(4 * c + 1 - line(2)).start()
        else:
            delta_copy(4 * c + 1 - r).start()
        sent.append(c)

    dall[r] = dsend[r]
    for i in range(1, m):
        finish(dall.at[0], delta_sem.at[1, line(i)])
    give(groups[1])

    def post(turn, to):
        remote(outbuf.at[to], landed.at[s], out_sem, (turn,), to, r).start()

    span = 2 * W * G
    for turn in turns:
        first = quarter(turn) * 2 * W
        part = mm(place_hot[pl.ds(pl.multiple_of(first * G, span), span)], dall[...].reshape(m * T, LANES))
        outbuf[pl.ds(first, 2 * W)] = part.astype(BF16).reshape(2 * W, G, LANES)
        if turn == turns[0]:
            scatter(first_lines, post)
    scatter(other_lines, post)
    landed[s] = outbuf[s]

    for i in range(1, m):
        finish(asked_all.at[0], ask_sem.at[1, i])
    fan_no = jnp.floor((iota((n, n * G), 1).astype(F32) + 0.5) * (1.0 / G))
    fan = one_hot(fan_no == iota((n, n * G), 0).astype(F32))
    lane_no = iota((2 * PAD, n * G), 1).astype(F32)
    seat = lane_no - jnp.floor((lane_no + 0.5) * (1.0 / G)) * float(G)
    line_no = iota((2 * PAD, n * G), 0)
    weight = jnp.where(line_no < PAD, 32.0, 1.0)
    seat_of = (line_no & (PAD - 1)).astype(F32)
    target = jnp.full((1, n * G), -1.0, F32)
    for q in range(m):
        turned = jnp.transpose(asked_all[q])[:2 * PAD].astype(BF16)
        values = mm(turned, fan) * weight
        here = (seat == seat_of + float(q * cap)) & (seat_of < float(cap))
        target = target + jnp.sum(jnp.where(here, values, 0.0), axis=0, keepdims=True)
    step = LANES

    def fill_owner(c, carry):
        at = pl.multiple_of(c * step, step)
        owner_hot[pl.ds(at, step)] = one_hot((iota((step, n * G), 0) + c * step).astype(F32) == target)
        return carry

    lax.fori_loop(0, R // step, fill_owner, 0)

    arrive(groups[1])
    others(groups[1], lambda ref, w, i: finish(ref, wc_sem.at[1, w, i]))
    query = mm(hn[...].astype(BF16), wq[...]).astype(BF16)
    keyval = mm(hd[...], wk[...]).astype(BF16)
    head = D // H
    blocks = E // BLK
    block_no = iota((BLK, E), 1) >> 7
    for q in range(blocks):
        times = sum((block_no == listed_ref[k:k + 1, q:q + 1]).astype(F32) for k in range(2))
        seen = times > 0.0
        for h in range(H):
            cols = slice(h * head, (h + 1) * head)
            at = slice(q * BLK, (q + 1) * BLK)
            scores = mm_nt(query[at, cols], keyval[:, cols]) * (1.0 / math.sqrt(head))
            scores = jnp.where(seen, scores, -jnp.inf)
            top = jnp.max(scores, axis=1, keepdims=True)
            weighed = jnp.exp(scores - top) * times
            prob = (weighed / jnp.sum(weighed, axis=1, keepdims=True)).astype(BF16)
            attend = mm(prob, keyval[:, D + h * head:D + (h + 1) * head])
            embed_ref[at, cols] = (hn[at, cols] + attend).astype(BF16)

    embed_copy = pltpu.make_async_copy(embed_ref, embed_hbm, local_sem.at[1])
    embed_copy.start()

    def cols_of(rep):
        return pl.ds(pl.multiple_of(rep * LANES, LANES), LANES)

    def landed_part(turn, lines):
        first = quarter(half - turn) * 2 * W
        hot = owner_hot[lines, pl.ds(pl.multiple_of(first * G, span), span)]
        return mm(hot, landed[pl.ds(first, 2 * W)].reshape(span, LANES))

    right, left = line(1), line(m - 1)
    for turn in turns[:-1]:
        finish(landed.at[pl.ds(0, group_size(turn))], out_sem.at[1, turn])
        part = landed_part(turn, slice(None))
        total[...] = part if turn == turns[0] else total[...] + part
    turn = turns[-1]
    finish(landed.at[pl.ds(0, group_size(turn))], out_sem.at[1, turn])
    step = R // CUTS

    def new_copy(kind, c, src, owner_rep, to):
        at = (pl.ds(c * step, step), cols_of(owner_rep))
        return remote(new_ref.at[at] if src is None else src, new_ref.at[at], new_sem, (kind, c), s, to)

    for c in range(CUTS):
        at = pl.ds(c * step, step)
        newcol[at] = (mem[at, cols_of(r)].astype(F32) + (total[at] + landed_part(turn, at))).astype(BF16)
        new_copy(0, c, newcol.at[at], r, right).start()
        new_copy(1, c, newcol.at[at], r, left).start()
    keep = pltpu.make_async_copy(newcol, new_ref.at[:, cols_of(r)], local_sem.at[0])
    keep.start()
    for c in range(CUTS):
        if c % 2 == 0:
            finish(newcol.at[pl.ds(0, step)], new_sem.at[1, 0, c])
            new_copy(2, c, None, left, right).start()
        else:
            finish(newcol.at[pl.ds(0, step)], new_sem.at[1, 1, c])
            new_copy(3, c, None, right, left).start()
    keep.wait()
    for c in range(CUTS):
        finish(newcol.at[pl.ds(0, step)], new_sem.at[1, 1 - c % 2, c])
        finish(newcol.at[pl.ds(0, step)], new_sem.at[1, 2 + c % 2, c])

    embed_copy.wait()
    finish(halfway.at[pl.ds(0, YS - 1)], req_sem.at[0, 0])
    finish(asked.at[:, pl.ds(0, W - 1)], req_sem.at[0, 1])
    for turn in turns:
        finish(rows.at[pl.ds(0, group_size(turn)), pl.ds(0, cap)], row_sem.at[0, turn])
        finish(landed.at[pl.ds(0, group_size(turn))], out_sem.at[0, turn])
    for c in range(CUTS):
        for kind in (0, 1, 2 + c % 2):
            finish(newcol.at[pl.ds(0, step)], new_sem.at[0, kind, c])
    for i in range(1, m):
        finish(slots_all.at[0], slot_sem.at[0, i])
        finish(asked_all.at[0], ask_sem.at[0, i])
        finish(dall.at[0], delta_sem.at[0, line(i)])
    for g in range(2):
        others(groups[g], lambda ref, w, i: finish(ref, wx_sem.at[0, w, i]))
        others(groups[g], lambda ref, w, i: finish(ref, wc_sem.at[0, w, i]))


def settle(embed_in, new_in, embed_out, new_out, embed_buf, new_buf, sems):
    moves = []
    for src, buf, dst, count in ((new_in, new_buf, new_out, 4), (embed_in, embed_buf, embed_out, 2)):
        size = src.shape[0] // count
        for c in range(count):
            at = pl.ds(c * size, size)
            k = len(moves)
            moves.append((
                pltpu.make_async_copy(src.at[at], buf.at[at], sems.at[0, k]),
                pltpu.make_async_copy(buf.at[at], dst.at[at], sems.at[1, k]),
            ))
            moves[-1][0].start()
    for come, go in moves:
        come.wait()
        go.start()
    for come, go in moves:
        go.wait()


def shards(
    memory, touch_owner, touch_row, touch_time, src_slot, dst_slot, event_time, neighbour_blocks,
    time_freq, time_phase, w_input, w_time, w_hidden, w_query, w_keyval,
):
    n = lax.axis_size("shard")
    m = lax.axis_size("rep")
    T = touch_row.shape[0]
    E = src_slot.shape[0]
    R, D = memory.shape
    cap = 2 * T // n + 2
    G = m * cap
    anywhere = pl.BlockSpec(memory_space=pl.ANY)
    weights = (w_input, w_time, w_hidden, w_query, w_keyval)
    dma = pltpu.SemaphoreType.DMA
    small = (
        touch_owner.reshape(1, T), touch_row.reshape(1, T), touch_time.reshape(1, T),
        src_slot, dst_slot, event_time,
        neighbour_blocks.T, time_freq.reshape(1, -1), time_phase.reshape(1, -1),
    )
    embed, new_memory = pl.pallas_call(
        functools.partial(body, n, m, cap),
        out_shape=(jax.ShapeDtypeStruct((E, D), BF16), jax.ShapeDtypeStruct((R, D), BF16)),
        in_specs=[anywhere] * 15,
        out_specs=(anywhere, anywhere),
        scratch_shapes=[pltpu.VMEM(x.shape, x.dtype) for x in small]
        + [dma((len(small),)), pltpu.VMEM((E, D), BF16), pltpu.VMEM((R, D), BF16)]
        + [pltpu.VMEM((w.shape[0], w.shape[1] * m), BF16) for w in weights]
        + [
            pltpu.VMEM((YS, n // YS, 1, LANES), F32),
            pltpu.VMEM((YS, n // YS, 1, LANES), F32),
            pltpu.VMEM((YS, n // YS, 1, LANES), F32),
            pltpu.VMEM((m, n, LANES), F32),
            pltpu.VMEM((m, 1, T), F32),
            pltpu.VMEM((n, PAD, D), BF16),
            pltpu.VMEM((n, PAD, D), BF16),
            pltpu.VMEM((n * G, m * T), BF16),
            pltpu.VMEM((R, n * G), BF16),
            pltpu.VMEM((E, D), BF16),
            pltpu.VMEM((E, D), BF16),
            pltpu.VMEM((E, D), F32),
            pltpu.VMEM((m, T, LANES), BF16),
            pltpu.VMEM((m, T, LANES), BF16),
            pltpu.VMEM((n, G, LANES), BF16),
            pltpu.VMEM((n, G, LANES), BF16),
            pltpu.VMEM((R, LANES), BF16),
            pltpu.VMEM((n * PAD, LANES), F32),
            pltpu.VMEM((T, n * PAD), BF16),
            pltpu.VMEM((R, LANES), F32),
            dma((6,)),
            dma((2, 2)),
            dma((2, m)),
            dma((2, m)),
            dma((2, len(weights), m)),
            dma((2, len(weights), m)),
            dma((2, YS // 2)),
            dma((2, m)),
            dma((2, YS // 2)),
            dma((2, 4, CUTS)),
        ],
        compiler_params=pltpu.CompilerParams(
            collective_id=0, has_side_effects=True, vmem_limit_bytes=56 * 1024 * 1024
        ),
    )(
        *small,
        memory, *weights,
    )
    return pl.pallas_call(
        settle,
        out_shape=(jax.ShapeDtypeStruct((E, D), BF16), jax.ShapeDtypeStruct((R, D), BF16)),
        in_specs=[anywhere] * 2,
        out_specs=(anywhere, anywhere),
        scratch_shapes=[pltpu.VMEM((E, D), BF16), pltpu.VMEM((R, D), BF16), dma((2, 6))],
        cost_estimate=pl.CostEstimate(flops=0, bytes_accessed=4 * (E + R) * D, transcendentals=0),
    )(embed, new_memory)


def solution(mesh):
    both = P(("shard", "rep"))
    placed = (
        P("shard", None), P(("shard", "rep"), None), both, both, both, both, both,
        P(("shard", "rep"), None), P(), P(),
    ) + (P(None, "rep"),) * 5
    return jax.shard_map(
        shards,
        mesh=mesh,
        in_specs=placed,
        out_specs=(P(("shard", "rep"), None), P("shard", None)),
        check_vma=False,
    )
```

```python
import functools
import math

import jax
import jax.numpy as jnp
from jax import lax
from jax.experimental import pallas as pl
from jax.experimental.pallas import tpu as pltpu
from jax.sharding import PartitionSpec as P

H = 4
BLK = 128
LANES = 128
PAD = 8
YS = 8
CUTS = 8
F32 = jnp.float32
BF16 = jnp.bfloat16
I32 = jnp.int32


def mm(a, b):
    return jnp.dot(a, b, preferred_element_type=F32)


def mm_nt(a, b):
    return lax.dot_general(a, b, (((1,), (1,)), ((), ())), preferred_element_type=F32)


def mm_tn(a, b):
    return lax.dot_general(a, b, (((0,), (0,)), ((), ())), preferred_element_type=F32)


def iota(shape, dim):
    return lax.broadcasted_iota(I32, shape, dim)


def one_hot(cond):
    return jnp.where(cond, 1.0, 0.0).astype(BF16)


def column(row):
    return jnp.transpose(jnp.broadcast_to(row, (LANES, row.shape[1])))


def rowhot(col, width):
    lane = iota(col.shape, 1).astype(F32)
    parts = [one_hot(col == lane + float(k * LANES)) for k in range(pl.cdiv(width, LANES))]
    hot = parts[0] if len(parts) == 1 else jnp.concatenate(parts, axis=1)
    return hot if hot.shape[1] == width else hot[:, :width]


def body(
    n, m, cap,
    *refs,
):
    small_hbm, refs = refs[:9], refs[9:]
    (
        mem_hbm, wi_hbm, wt_hbm, wh_hbm, wq_hbm, wk_hbm, embed_hbm, new_ref,
    ), refs = refs[:8], refs[8:]
    small, small_sem, embed_ref, refs = refs[:9], refs[9], refs[10], refs[11:]
    owner_ref, row_ref, tick_ref, src_ref, dst_ref, stamp_ref, listed_ref, freq_ref, phase_ref = small
    (
    mem, wi, wt, wh, wq, wk,
    reqbuf, halfway, asked, asked_all, slots_all, served, rows, place_hot, owner_hot,
    hs, hd, hn, dsend, dall, outbuf, landed, newcol, slot_hot, total,
    local_sem, req_sem, slot_sem, ask_sem, wx_sem, wc_sem, row_sem, delta_sem, out_sem, new_sem,
    ) = refs
    s = lax.axis_index("shard")
    r = lax.axis_index("rep")
    T = owner_ref.shape[1]
    E = src_ref.shape[0]
    R, D = mem.shape
    G = m * cap
    W = n // YS
    core = lax.rem(s, 2)
    sibling = s + 1 - 2 * core

    def line(i):
        return lax.rem(r + i, m)

    def remote(src, dst, sems, at, shard, rep):
        return pltpu.make_async_remote_copy(
            src_ref=src, dst_ref=dst, send_sem=sems.at[(0,) + at], recv_sem=sems.at[(1,) + at],
            device_id=(shard, rep), device_id_type=pl.DeviceIdType.MESH,
        )

    def finish(ref, sem):
        pltpu.make_async_copy(ref, ref, sem).wait()

    small_copies = [
        pltpu.make_async_copy(src, dst, small_sem.at[k]) for k, (src, dst) in enumerate(zip(small_hbm, small))
    ]
    for copy in small_copies:
        copy.start()
    weights = ((wi_hbm, wi), (wt_hbm, wt), (wh_hbm, wh), (wq_hbm, wq), (wk_hbm, wk))
    barrier = pltpu.get_barrier_semaphore()

    yy = s // W
    ww = lax.rem(s, W)

    def signal(sem, shard, rep):
        pl.semaphore_signal(sem, inc=1, device_id=(shard, rep), device_id_type=pl.DeviceIdType.MESH)

    for i in range(1, YS):
        signal(barrier, lax.rem(yy + i, YS) * W + ww, r)

    def greet(i, carry):
        signal(barrier, yy * W + lax.rem(ww + i, W), r)
        return carry

    lax.fori_loop(1, W, greet, 0)
    for i in range(1, m):
        signal(barrier, s, line(i))
    rows[...] = jnp.zeros_like(rows)

    half = YS // 2
    turns = (2, 1, 3, 0)

    def quarter(turn):
        return lax.rem(yy // 2 + turn, half)

    def scatter(lines, send):
        def pick(q, carry):
            for k, (turn, which) in enumerate(lines):
                at = lax.rem(ww + q * 5 + k * 3 + W // 2, W)
                to = (quarter(turn) * 2 + which) * W + at
                if turn:
                    send(turn, to)
                else:
                    pl.when(to != s)(lambda: send(turn, to))
            return carry

        lax.fori_loop(0, W, pick, 0)

    first_lines = ((2, 0), (2, 1))
    other_lines = ((1, 1), (3, 0), (1, 0), (3, 1), (0, 0), (0, 1))

    def group_size(turn):
        return 2 * W if turn else 2 * W - 1

    for copy in small_copies[:2]:
        copy.wait()
    owner = owner_ref[...]
    hit = one_hot(iota((n, T), 0) == owner)
    earlier = one_hot(iota((T, T), 0) < iota((T, T), 1))
    place = jnp.sum(mm(hit, earlier) * hit.astype(F32), axis=0, keepdims=True)
    asked_row = row_ref[...] + 1
    line_at = iota((LANES, T), 0).astype(F32)
    ask_hi = (asked_row >> 5).astype(F32)
    ask_lo = (asked_row & 31).astype(F32)
    table = jnp.where(line_at == place, ask_hi, jnp.where(line_at == place + float(PAD), ask_lo, 0.0))
    reqbuf[...] = mm_nt(hit, table.astype(BF16)).reshape(YS, W, 1, LANES)
    ownerf = owner.astype(F32)
    slots_all[r] = ownerf * float(G) + place + (r * cap).astype(F32)
    halfway[yy] = reqbuf[yy]

    pl.semaphore_wait(barrier, YS - 1 + W - 1 + m - 1)

    for i in range(1, YS):
        y = lax.rem(yy + i, YS)
        remote(reqbuf.at[y], halfway.at[yy], req_sem, (0,), y * W + ww, r).start()
    mem_copy = pltpu.make_async_copy(mem_hbm, mem, local_sem.at[0])
    mem_copy.start()
    own = []
    for at, (shard_ref, full) in enumerate(weights):
        width = shard_ref.shape[1]
        copy = pltpu.make_async_copy(
            shard_ref, full.at[:, pl.ds(pl.multiple_of(r * width, LANES), width)], local_sem.at[1 + at]
        )
        copy.start()
        own.append(copy)
    finish(halfway.at[pl.ds(0, YS - 1)], req_sem.at[1, 0])

    def ask(i, carry):
        w = lax.rem(ww + i, W)
        remote(halfway.at[:, w], asked.at[:, ww], req_sem, (1,), yy * W + w, r).start()
        return carry

    lax.fori_loop(1, W, ask, 0)
    asked[:, ww] = halfway[:, ww]
    for i in range(1, m):
        remote(slots_all.at[r], slots_all.at[r], slot_sem, (i,), s, line(i)).start()

    def halves(group):
        out = []
        for w in group:
            shard_ref, full = weights[w]
            depth, width = shard_ref.shape
            half = depth // 2
            out.append((w, shard_ref, full, pl.ds(pl.multiple_of(core * half, PAD), half), width))
        return out

    groups = ((1, 2, 0), (3, 4))

    def give(group):
        for i in range(1, m):
            for w, shard_ref, full, part, width in halves(group):
                cols = pl.ds(pl.multiple_of(r * width, LANES), width)
                remote(shard_ref.at[part], full.at[part, cols], wx_sem, (w, i), s, line(i)).start()

    give(groups[0])

    finish(asked.at[:, pl.ds(0, W - 1)], req_sem.at[1, 1])
    table_in = asked[...].reshape(n, LANES)
    table_in = table_in.astype(BF16)
    depth_at = iota((LANES, LANES), 0)
    scale = jnp.where(depth_at < PAD, 32.0, jnp.where(depth_at < 2 * PAD, 1.0, 0.0)).astype(BF16)
    piece = 2 * W * PAD
    lane = iota((piece, LANES), 1)
    mine = ((lane & (PAD - 1)) == (iota((piece, LANES), 0) & (PAD - 1))) & (lane < 2 * PAD)
    mem_copy.wait()

    def serve(turn, to):
        remote(served.at[to, pl.ds(0, cap)], rows.at[s, pl.ds(0, cap)], row_sem, (turn,), to, r).start()

    for turn in turns:
        first = quarter(turn) * 2 * W
        spread = one_hot((iota((piece, n), 0) >> 3) + first == iota((piece, n), 1))
        picked = jnp.where(mine, mm(spread, table_in), 0.0).astype(BF16)
        hot = rowhot(mm(picked, scale) - 1.0, R)
        served[pl.ds(first, 2 * W)] = mm(hot, mem[...]).astype(BF16).reshape(2 * W, PAD, D)
        if turn == turns[0]:
            scatter(first_lines, serve)
    scatter(other_lines, serve)
    rows[s] = served[s]
    asked_all[r] = asked[...].reshape(n, LANES)
    for i in range(1, m):
        remote(asked_all.at[r], asked_all.at[r], ask_sem, (i,), s, line(i)).start()

    for copy in small_copies[2:]:
        copy.wait()
    src_row = src_ref[...].reshape(1, E).astype(F32)
    src_hot = rowhot(column(src_row), T)
    dst_hot = rowhot(column(dst_ref[...].reshape(1, E).astype(F32)), T)
    src_hot_t = one_hot(iota((T, E), 0).astype(F32) == src_row)
    slot_hot[...] = rowhot(column(ownerf * float(PAD) + place), n * PAD)
    counts = mm(src_hot_t, jnp.ones((E, LANES), BF16))
    share = 1.0 / jnp.maximum(counts, 1.0)
    tick = tick_ref[...]
    tick_hi = column((tick >> 5).astype(F32)).astype(BF16)
    tick_lo = column((tick & 31).astype(F32)).astype(BF16)
    ticks = mm(src_hot, tick_hi) * 32.0 + mm(src_hot, tick_lo)
    spans = column(stamp_ref[...].reshape(1, E).astype(F32)) - ticks
    encode = jnp.cos(spans * freq_ref[...] + phase_ref[...]).astype(BF16)

    for i in range(1, m):
        finish(slots_all.at[0], slot_sem.at[1, i])
    rung = min(n * G, 384)

    def fill_place(c, carry):
        at = pl.multiple_of(c * rung, rung)
        line_no = (iota((rung, T), 0) + c * rung).astype(F32)
        for q in range(m):
            place_hot[pl.ds(at, rung), pl.ds(q * T, T)] = one_hot(line_no == slots_all[q])
        return carry

    lax.fori_loop(0, n * G // rung, fill_place, 0)

    for copy in own:
        copy.wait()

    def others(group, do):
        for i in range(1, m):
            for w, shard_ref, full, part, width in halves(group):
                cols = pl.ds(pl.multiple_of(line(i) * width, LANES), width)
                do(full.at[part, cols], w, i)

    def arrive(group):
        others(group, lambda ref, w, i: finish(ref, wx_sem.at[1, w, m - i]))
        others(group, lambda ref, w, i: remote(ref, ref, wc_sem, (w, i), sibling, r).start())

    arrive(groups[0])

    fetched = jnp.zeros((T, D), F32)
    for turn in turns:
        finish(rows.at[pl.ds(0, group_size(turn)), pl.ds(0, cap)], row_sem.at[1, turn])
        first = quarter(half - turn) * 2 * W
        came = slot_hot[:, pl.ds(pl.multiple_of(first * PAD, piece), piece)]
        fetched = fetched + mm(came, rows[pl.ds(first, 2 * W)].reshape(piece, D))
    fetched = fetched.astype(BF16)
    hs[...] = mm(src_hot, fetched).astype(BF16)
    hd[...] = mm(dst_hot, fetched).astype(BF16)
    others(groups[0], lambda ref, w, i: finish(ref, wc_sem.at[1, w, i]))
    wide = 2 * LANES
    sent = []

    def delta_copy(to):
        return pltpu.make_async_remote_copy(
            src_ref=dsend.at[to], dst_ref=dall.at[r], send_sem=delta_sem.at[0, to], recv_sem=delta_sem.at[1, r],
            device_id=(s, to), device_id_type=pl.DeviceIdType.MESH,
        )

    for c in (1 - r // 2, r // 2):
        here = pl.ds(pl.multiple_of(c * wide, wide), wide)

        def gate(k):
            return pl.ds(pl.multiple_of(k * D + c * wide, wide), wide)

        reset = mm(hd[...], wi[:, gate(0)]) + mm(encode, wt[:, gate(0)]) + mm(hs[...], wh[:, gate(0)])
        update = mm(hd[...], wi[:, gate(1)]) + mm(encode, wt[:, gate(1)]) + mm(hs[...], wh[:, gate(1)])
        reset = 0.5 * jnp.tanh(0.5 * reset) + 0.5
        update = 0.5 * jnp.tanh(0.5 * update) + 0.5
        fresh = jnp.tanh(
            mm(hd[...], wi[:, gate(2)]) + mm(encode, wt[:, gate(2)]) + reset * mm(hs[...], wh[:, gate(2)])
        )
        hold = hs[:, here].astype(F32)
        change = (1.0 - update) * (fresh - hold)
        hn[:, here] = hold + change
        delta = mm(src_hot_t, change.astype(BF16))
        for k in range(2):
            dsend[2 * c + k] = (delta[:, k * LANES:(k + 1) * LANES] * share).astype(BF16)
        if not sent:
            delta_copy(line(2)).start()
            delta_copy(4 * c + 1 - line(2)).start()
        else:
            delta_copy(4 * c + 1 - r).start()
        sent.append(c)

    dall[r] = dsend[r]
    for i in range(1, m):
        finish(dall.at[0], delta_sem.at[1, line(i)])

    def post(turn, to):
        remote(outbuf.at[to], landed.at[s], out_sem, (turn,), to, r).start()

    span = 2 * W * G
    for turn in turns:
        first = quarter(turn) * 2 * W
        part = mm(place_hot[pl.ds(pl.multiple_of(first * G, span), span)], dall[...].reshape(m * T, LANES))
        outbuf[pl.ds(first, 2 * W)] = part.astype(BF16).reshape(2 * W, G, LANES)
        if turn == turns[0]:
            scatter(first_lines, post)
    scatter(other_lines, post)
    give(groups[1])
    landed[s] = outbuf[s]

    for i in range(1, m):
        finish(asked_all.at[0], ask_sem.at[1, i])
    fan_no = jnp.floor((iota((n, n * G), 1).astype(F32) + 0.5) * (1.0 / G))
    fan = one_hot(fan_no == iota((n, n * G), 0).astype(F32))
    lane_no = iota((2 * PAD, n * G), 1).astype(F32)
    seat = lane_no - jnp.floor((lane_no + 0.5) * (1.0 / G)) * float(G)
    line_no = iota((2 * PAD, n * G), 0)
    weight = jnp.where(line_no < PAD, 32.0, 1.0)
    seat_of = (line_no & (PAD - 1)).astype(F32)
    target = jnp.full((1, n * G), -1.0, F32)
    for q in range(m):
        turned = jnp.transpose(asked_all[q])[:2 * PAD].astype(BF16)
        values = mm(turned, fan) * weight
        here = (seat == seat_of + float(q * cap)) & (seat_of < float(cap))
        target = target + jnp.sum(jnp.where(here, values, 0.0), axis=0, keepdims=True)
    step = LANES

    def fill_owner(c, carry):
        at = pl.multiple_of(c * step, step)
        owner_hot[pl.ds(at, step)] = one_hot((iota((step, n * G), 0) + c * step).astype(F32) == target)
        return carry

    lax.fori_loop(0, R // step, fill_owner, 0)

    arrive(groups[1])
    others(groups[1], lambda ref, w, i: finish(ref, wc_sem.at[1, w, i]))
    query = mm(hn[...].astype(BF16), wq[...]).astype(BF16)
    keyval = mm(hd[...], wk[...]).astype(BF16)
    head = D // H
    blocks = E // BLK
    block_no = iota((BLK, E), 1) >> 7
    for q in range(blocks):
        times = sum((block_no == listed_ref[k:k + 1, q:q + 1]).astype(F32) for k in range(2))
        seen = times > 0.0
        for h in range(H):
            cols = slice(h * head, (h + 1) * head)
            at = slice(q * BLK, (q + 1) * BLK)
            scores = mm_nt(query[at, cols], keyval[:, cols]) * (1.0 / math.sqrt(head))
            scores = jnp.where(seen, scores, -jnp.inf)
            top = jnp.max(scores, axis=1, keepdims=True)
            weighed = jnp.exp(scores - top) * times
            prob = (weighed / jnp.sum(weighed, axis=1, keepdims=True)).astype(BF16)
            attend = mm(prob, keyval[:, D + h * head:D + (h + 1) * head])
            embed_ref[at, cols] = (hn[at, cols] + attend).astype(BF16)

    embed_copy = pltpu.make_async_copy(embed_ref, embed_hbm, local_sem.at[1])
    embed_copy.start()

    def cols_of(rep):
        return pl.ds(pl.multiple_of(rep * LANES, LANES), LANES)

    def landed_part(turn, lines):
        first = quarter(half - turn) * 2 * W
        hot = owner_hot[lines, pl.ds(pl.multiple_of(first * G, span), span)]
        return mm(hot, landed[pl.ds(first, 2 * W)].reshape(span, LANES))

    right, left = line(1), line(m - 1)
    for turn in turns[:-1]:
        finish(landed.at[pl.ds(0, group_size(turn))], out_sem.at[1, turn])
        part = landed_part(turn, slice(None))
        total[...] = part if turn == turns[0] else total[...] + part
    turn = turns[-1]
    finish(landed.at[pl.ds(0, group_size(turn))], out_sem.at[1, turn])
    step = R // CUTS

    def new_copy(kind, c, src, owner_rep, to):
        at = (pl.ds(c * step, step), cols_of(owner_rep))
        return remote(new_ref.at[at] if src is None else src, new_ref.at[at], new_sem, (kind, c), s, to)

    for c in range(CUTS):
        at = pl.ds(c * step, step)
        newcol[at] = (mem[at, cols_of(r)].astype(F32) + (total[at] + landed_part(turn, at))).astype(BF16)
        new_copy(0, c, newcol.at[at], r, right).start()
        new_copy(1, c, newcol.at[at], r, left).start()
    keep = pltpu.make_async_copy(newcol, new_ref.at[:, cols_of(r)], local_sem.at[0])
    keep.start()
    for c in range(CUTS):
        if c % 2 == 0:
            finish(newcol.at[pl.ds(0, step)], new_sem.at[1, 0, c])
            new_copy(2, c, None, left, right).start()
        else:
            finish(newcol.at[pl.ds(0, step)], new_sem.at[1, 1, c])
            new_copy(3, c, None, right, left).start()
    keep.wait()
    for c in range(CUTS):
        finish(newcol.at[pl.ds(0, step)], new_sem.at[1, 1 - c % 2, c])
        finish(newcol.at[pl.ds(0, step)], new_sem.at[1, 2 + c % 2, c])

    embed_copy.wait()
    finish(halfway.at[pl.ds(0, YS - 1)], req_sem.at[0, 0])
    finish(asked.at[:, pl.ds(0, W - 1)], req_sem.at[0, 1])
    for turn in turns:
        finish(rows.at[pl.ds(0, group_size(turn)), pl.ds(0, cap)], row_sem.at[0, turn])
        finish(landed.at[pl.ds(0, group_size(turn))], out_sem.at[0, turn])
    for c in range(CUTS):
        for kind in (0, 1, 2 + c % 2):
            finish(newcol.at[pl.ds(0, step)], new_sem.at[0, kind, c])
    for i in range(1, m):
        finish(slots_all.at[0], slot_sem.at[0, i])
        finish(asked_all.at[0], ask_sem.at[0, i])
        finish(dall.at[0], delta_sem.at[0, line(i)])
    for g in range(2):
        others(groups[g], lambda ref, w, i: finish(ref, wx_sem.at[0, w, i]))
        others(groups[g], lambda ref, w, i: finish(ref, wc_sem.at[0, w, i]))


def settle(embed_in, new_in, embed_out, new_out, embed_buf, new_buf, sems):
    moves = []
    for src, buf, dst, count in ((new_in, new_buf, new_out, 4), (embed_in, embed_buf, embed_out, 2)):
        size = src.shape[0] // count
        for c in range(count):
            at = pl.ds(c * size, size)
            k = len(moves)
            moves.append((
                pltpu.make_async_copy(src.at[at], buf.at[at], sems.at[0, k]),
                pltpu.make_async_copy(buf.at[at], dst.at[at], sems.at[1, k]),
            ))
            moves[-1][0].start()
    for come, go in moves:
        come.wait()
        go.start()
    for come, go in moves:
        go.wait()


def shards(
    memory, touch_owner, touch_row, touch_time, src_slot, dst_slot, event_time, neighbour_blocks,
    time_freq, time_phase, w_input, w_time, w_hidden, w_query, w_keyval,
):
    n = lax.axis_size("shard")
    m = lax.axis_size("rep")
    T = touch_row.shape[0]
    E = src_slot.shape[0]
    R, D = memory.shape
    cap = 2 * T // n + 2
    G = m * cap
    anywhere = pl.BlockSpec(memory_space=pl.ANY)
    weights = (w_input, w_time, w_hidden, w_query, w_keyval)
    dma = pltpu.SemaphoreType.DMA
    small = (
        touch_owner.reshape(1, T), touch_row.reshape(1, T), touch_time.reshape(1, T),
        src_slot, dst_slot, event_time,
        neighbour_blocks.T, time_freq.reshape(1, -1), time_phase.reshape(1, -1),
    )
    embed, new_memory = pl.pallas_call(
        functools.partial(body, n, m, cap),
        out_shape=(jax.ShapeDtypeStruct((E, D), BF16), jax.ShapeDtypeStruct((R, D), BF16)),
        in_specs=[anywhere] * 15,
        out_specs=(anywhere, anywhere),
        scratch_shapes=[pltpu.VMEM(x.shape, x.dtype) for x in small]
        + [dma((len(small),)), pltpu.VMEM((E, D), BF16), pltpu.VMEM((R, D), BF16)]
        + [pltpu.VMEM((w.shape[0], w.shape[1] * m), BF16) for w in weights]
        + [
            pltpu.VMEM((YS, n // YS, 1, LANES), F32),
            pltpu.VMEM((YS, n // YS, 1, LANES), F32),
            pltpu.VMEM((YS, n // YS, 1, LANES), F32),
            pltpu.VMEM((m, n, LANES), F32),
            pltpu.VMEM((m, 1, T), F32),
            pltpu.VMEM((n, PAD, D), BF16),
            pltpu.VMEM((n, PAD, D), BF16),
            pltpu.VMEM((n * G, m * T), BF16),
            pltpu.VMEM((R, n * G), BF16),
            pltpu.VMEM((E, D), BF16),
            pltpu.VMEM((E, D), BF16),
            pltpu.VMEM((E, D), F32),
            pltpu.VMEM((m, T, LANES), BF16),
            pltpu.VMEM((m, T, LANES), BF16),
            pltpu.VMEM((n, G, LANES), BF16),
            pltpu.VMEM((n, G, LANES), BF16),
            pltpu.VMEM((R, LANES), BF16),
            pltpu.VMEM((T, n * PAD), BF16),
            pltpu.VMEM((R, LANES), F32),
            dma((6,)),
            dma((2, 2)),
            dma((2, m)),
            dma((2, m)),
            dma((2, len(weights), m)),
            dma((2, len(weights), m)),
            dma((2, YS // 2)),
            dma((2, m)),
            dma((2, YS // 2)),
            dma((2, 4, CUTS)),
        ],
        compiler_params=pltpu.CompilerParams(
            collective_id=0, has_side_effects=True, vmem_limit_bytes=56 * 1024 * 1024
        ),
    )(
        *small,
        memory, *weights,
    )
    return pl.pallas_call(
        settle,
        out_shape=(jax.ShapeDtypeStruct((E, D), BF16), jax.ShapeDtypeStruct((R, D), BF16)),
        in_specs=[anywhere] * 2,
        out_specs=(anywhere, anywhere),
        scratch_shapes=[pltpu.VMEM((E, D), BF16), pltpu.VMEM((R, D), BF16), dma((2, 6))],
        cost_estimate=pl.CostEstimate(flops=0, bytes_accessed=4 * (E + R) * D, transcendentals=0),
    )(embed, new_memory)


def solution(mesh):
    both = P(("shard", "rep"))
    placed = (
        P("shard", None), P(("shard", "rep"), None), both, both, both, both, both,
        P(("shard", "rep"), None), P(), P(),
    ) + (P(None, "rep"),) * 5
    return jax.shard_map(
        shards,
        mesh=mesh,
        in_specs=placed,
        out_specs=(P(("shard", "rep"), None), P("shard", None)),
        check_vma=False,
    )
```

```python
import functools
import math

import jax
import jax.numpy as jnp
from jax import lax
from jax.experimental import pallas as pl
from jax.experimental.pallas import tpu as pltpu
from jax.sharding import PartitionSpec as P

H = 4
BLK = 128
LANES = 128
PAD = 8
YS = 8
CUTS = 16
F32 = jnp.float32
BF16 = jnp.bfloat16
I32 = jnp.int32


def mm(a, b):
    return jnp.dot(a, b, preferred_element_type=F32)


def mm_nt(a, b):
    return lax.dot_general(a, b, (((1,), (1,)), ((), ())), preferred_element_type=F32)


def mm_tn(a, b):
    return lax.dot_general(a, b, (((0,), (0,)), ((), ())), preferred_element_type=F32)


def iota(shape, dim):
    return lax.broadcasted_iota(I32, shape, dim)


def one_hot(cond):
    return jnp.where(cond, 1.0, 0.0).astype(BF16)


def column(row):
    return jnp.transpose(jnp.broadcast_to(row, (LANES, row.shape[1])))


def rowhot(col, width):
    lane = iota(col.shape, 1).astype(F32)
    parts = [one_hot(col == lane + float(k * LANES)) for k in range(pl.cdiv(width, LANES))]
    hot = parts[0] if len(parts) == 1 else jnp.concatenate(parts, axis=1)
    return hot if hot.shape[1] == width else hot[:, :width]


def body(
    n, m, cap,
    *refs,
):
    small_hbm, refs = refs[:9], refs[9:]
    (
        mem_hbm, wi_hbm, wt_hbm, wh_hbm, wq_hbm, wk_hbm, embed_hbm, new_ref,
    ), refs = refs[:8], refs[8:]
    small, small_sem, embed_ref, refs = refs[:9], refs[9], refs[10], refs[11:]
    owner_ref, row_ref, tick_ref, src_ref, dst_ref, stamp_ref, listed_ref, freq_ref, phase_ref = small
    (
    mem, wi, wt, wh, wq, wk,
    reqbuf, halfway, asked, asked_all, slots_all, served, rows, place_hot, owner_hot,
    hs, hd, hn, dsend, dall, outbuf, landed, newcol, slot_hot, total,
    local_sem, req_sem, slot_sem, ask_sem, wx_sem, wc_sem, row_sem, delta_sem, out_sem, new_sem,
    ) = refs
    s = lax.axis_index("shard")
    r = lax.axis_index("rep")
    T = owner_ref.shape[1]
    E = src_ref.shape[0]
    R, D = mem.shape
    G = m * cap
    W = n // YS
    core = lax.rem(s, 2)
    sibling = s + 1 - 2 * core

    def line(i):
        return lax.rem(r + i, m)

    def remote(src, dst, sems, at, shard, rep):
        return pltpu.make_async_remote_copy(
            src_ref=src, dst_ref=dst, send_sem=sems.at[(0,) + at], recv_sem=sems.at[(1,) + at],
            device_id=(shard, rep), device_id_type=pl.DeviceIdType.MESH,
        )

    def finish(ref, sem):
        pltpu.make_async_copy(ref, ref, sem).wait()

    small_copies = [
        pltpu.make_async_copy(src, dst, small_sem.at[k]) for k, (src, dst) in enumerate(zip(small_hbm, small))
    ]
    for copy in small_copies:
        copy.start()
    weights = ((wi_hbm, wi), (wt_hbm, wt), (wh_hbm, wh), (wq_hbm, wq), (wk_hbm, wk))
    barrier = pltpu.get_barrier_semaphore()

    yy = s // W
    ww = lax.rem(s, W)

    def signal(sem, shard, rep):
        pl.semaphore_signal(sem, inc=1, device_id=(shard, rep), device_id_type=pl.DeviceIdType.MESH)

    for i in range(1, YS):
        signal(barrier, lax.rem(yy + i, YS) * W + ww, r)

    def greet(i, carry):
        signal(barrier, yy * W + lax.rem(ww + i, W), r)
        return carry

    lax.fori_loop(1, W, greet, 0)
    for i in range(1, m):
        signal(barrier, s, line(i))
    rows[...] = jnp.zeros_like(rows)

    half = YS // 2
    turns = (2, 1, 3, 0)

    def quarter(turn):
        return lax.rem(yy // 2 + turn, half)

    def scatter(lines, send):
        def pick(q, carry):
            for k, (turn, which) in enumerate(lines):
                at = lax.rem(ww + q * 5 + k * 3 + W // 2, W)
                to = (quarter(turn) * 2 + which) * W + at
                if turn:
                    send(turn, to)
                else:
                    pl.when(to != s)(lambda: send(turn, to))
            return carry

        lax.fori_loop(0, W, pick, 0)

    first_lines = ((2, 0), (2, 1))
    other_lines = ((1, 1), (3, 0), (1, 0), (3, 1), (0, 0), (0, 1))

    def group_size(turn):
        return 2 * W if turn else 2 * W - 1

    for copy in small_copies[:2]:
        copy.wait()
    owner = owner_ref[...]
    hit = one_hot(iota((n, T), 0) == owner)
    earlier = one_hot(iota((T, T), 0) < iota((T, T), 1))
    place = jnp.sum(mm(hit, earlier) * hit.astype(F32), axis=0, keepdims=True)
    asked_row = row_ref[...] + 1
    line_at = iota((LANES, T), 0).astype(F32)
    ask_hi = (asked_row >> 5).astype(F32)
    ask_lo = (asked_row & 31).astype(F32)
    table = jnp.where(line_at == place, ask_hi, jnp.where(line_at == place + float(PAD), ask_lo, 0.0))
    reqbuf[...] = mm_nt(hit, table.astype(BF16)).reshape(YS, W, 1, LANES)
    ownerf = owner.astype(F32)
    slots_all[r] = ownerf * float(G) + place + (r * cap).astype(F32)
    halfway[yy] = reqbuf[yy]

    pl.semaphore_wait(barrier, YS - 1 + W - 1 + m - 1)

    for i in range(1, YS):
        y = lax.rem(yy + i, YS)
        remote(reqbuf.at[y], halfway.at[yy], req_sem, (0,), y * W + ww, r).start()
    mem_copy = pltpu.make_async_copy(mem_hbm, mem, local_sem.at[0])
    mem_copy.start()
    own = []
    for at, (shard_ref, full) in enumerate(weights):
        width = shard_ref.shape[1]
        copy = pltpu.make_async_copy(
            shard_ref, full.at[:, pl.ds(pl.multiple_of(r * width, LANES), width)], local_sem.at[1 + at]
        )
        copy.start()
        own.append(copy)
    finish(halfway.at[pl.ds(0, YS - 1)], req_sem.at[1, 0])

    def ask(i, carry):
        w = lax.rem(ww + i, W)
        remote(halfway.at[:, w], asked.at[:, ww], req_sem, (1,), yy * W + w, r).start()
        return carry

    lax.fori_loop(1, W, ask, 0)
    asked[:, ww] = halfway[:, ww]
    for i in range(1, m):
        remote(slots_all.at[r], slots_all.at[r], slot_sem, (i,), s, line(i)).start()

    def halves(group):
        out = []
        for w in group:
            shard_ref, full = weights[w]
            depth, width = shard_ref.shape
            half = depth // 2
            out.append((w, shard_ref, full, pl.ds(pl.multiple_of(core * half, PAD), half), width))
        return out

    groups = ((1, 2, 0), (3, 4))

    def give(group):
        for i in range(1, m):
            for w, shard_ref, full, part, width in halves(group):
                cols = pl.ds(pl.multiple_of(r * width, LANES), width)
                remote(shard_ref.at[part], full.at[part, cols], wx_sem, (w, i), s, line(i)).start()

    give(groups[0])

    finish(asked.at[:, pl.ds(0, W - 1)], req_sem.at[1, 1])
    table_in = asked[...].reshape(n, LANES)
    table_in = table_in.astype(BF16)
    depth_at = iota((LANES, LANES), 0)
    scale = jnp.where(depth_at < PAD, 32.0, jnp.where(depth_at < 2 * PAD, 1.0, 0.0)).astype(BF16)
    piece = 2 * W * PAD
    lane = iota((piece, LANES), 1)
    mine = ((lane & (PAD - 1)) == (iota((piece, LANES), 0) & (PAD - 1))) & (lane < 2 * PAD)
    mem_copy.wait()

    def serve(turn, to):
        remote(served.at[to, pl.ds(0, cap)], rows.at[s, pl.ds(0, cap)], row_sem, (turn,), to, r).start()

    for turn in turns:
        first = quarter(turn) * 2 * W
        spread = one_hot((iota((piece, n), 0) >> 3) + first == iota((piece, n), 1))
        picked = jnp.where(mine, mm(spread, table_in), 0.0).astype(BF16)
        hot = rowhot(mm(picked, scale) - 1.0, R)
        served[pl.ds(first, 2 * W)] = mm(hot, mem[...]).astype(BF16).reshape(2 * W, PAD, D)
        if turn == turns[0]:
            scatter(first_lines, serve)
    scatter(other_lines, serve)
    rows[s] = served[s]
    asked_all[r] = asked[...].reshape(n, LANES)
    for i in range(1, m):
        remote(asked_all.at[r], asked_all.at[r], ask_sem, (i,), s, line(i)).start()

    for copy in small_copies[2:]:
        copy.wait()
    src_row = src_ref[...].reshape(1, E).astype(F32)
    src_hot = rowhot(column(src_row), T)
    dst_hot = rowhot(column(dst_ref[...].reshape(1, E).astype(F32)), T)
    src_hot_t = one_hot(iota((T, E), 0).astype(F32) == src_row)
    slot_hot[...] = rowhot(column(ownerf * float(PAD) + place), n * PAD)
    counts = mm(src_hot_t, jnp.ones((E, LANES), BF16))
    share = 1.0 / jnp.maximum(counts, 1.0)
    tick = tick_ref[...]
    tick_hi = column((tick >> 5).astype(F32)).astype(BF16)
    tick_lo = column((tick & 31).astype(F32)).astype(BF16)
    ticks = mm(src_hot, tick_hi) * 32.0 + mm(src_hot, tick_lo)
    spans = column(stamp_ref[...].reshape(1, E).astype(F32)) - ticks
    encode = jnp.cos(spans * freq_ref[...] + phase_ref[...]).astype(BF16)

    for i in range(1, m):
        finish(slots_all.at[0], slot_sem.at[1, i])
    rung = min(n * G, 384)

    def fill_place(c, carry):
        at = pl.multiple_of(c * rung, rung)
        line_no = (iota((rung, T), 0) + c * rung).astype(F32)
        for q in range(m):
            place_hot[pl.ds(at, rung), pl.ds(q * T, T)] = one_hot(line_no == slots_all[q])
        return carry

    lax.fori_loop(0, n * G // rung, fill_place, 0)

    for copy in own:
        copy.wait()

    def others(group, do):
        for i in range(1, m):
            for w, shard_ref, full, part, width in halves(group):
                cols = pl.ds(pl.multiple_of(line(i) * width, LANES), width)
                do(full.at[part, cols], w, i)

    def arrive(group):
        others(group, lambda ref, w, i: finish(ref, wx_sem.at[1, w, m - i]))
        others(group, lambda ref, w, i: remote(ref, ref, wc_sem, (w, i), sibling, r).start())

    arrive(groups[0])

    fetched = jnp.zeros((T, D), F32)
    for turn in turns:
        finish(rows.at[pl.ds(0, group_size(turn)), pl.ds(0, cap)], row_sem.at[1, turn])
        first = quarter(half - turn) * 2 * W
        came = slot_hot[:, pl.ds(pl.multiple_of(first * PAD, piece), piece)]
        fetched = fetched + mm(came, rows[pl.ds(first, 2 * W)].reshape(piece, D))
    fetched = fetched.astype(BF16)
    hs[...] = mm(src_hot, fetched).astype(BF16)
    hd[...] = mm(dst_hot, fetched).astype(BF16)
    others(groups[0], lambda ref, w, i: finish(ref, wc_sem.at[1, w, i]))
    wide = 2 * LANES
    sent = []

    def delta_copy(to):
        return pltpu.make_async_remote_copy(
            src_ref=dsend.at[to], dst_ref=dall.at[r], send_sem=delta_sem.at[0, to], recv_sem=delta_sem.at[1, r],
            device_id=(s, to), device_id_type=pl.DeviceIdType.MESH,
        )

    for c in (1 - r // 2, r // 2):
        here = pl.ds(pl.multiple_of(c * wide, wide), wide)

        def gate(k):
            return pl.ds(pl.multiple_of(k * D + c * wide, wide), wide)

        reset = mm(hd[...], wi[:, gate(0)]) + mm(encode, wt[:, gate(0)]) + mm(hs[...], wh[:, gate(0)])
        update = mm(hd[...], wi[:, gate(1)]) + mm(encode, wt[:, gate(1)]) + mm(hs[...], wh[:, gate(1)])
        reset = 0.5 * jnp.tanh(0.5 * reset) + 0.5
        update = 0.5 * jnp.tanh(0.5 * update) + 0.5
        fresh = jnp.tanh(
            mm(hd[...], wi[:, gate(2)]) + mm(encode, wt[:, gate(2)]) + reset * mm(hs[...], wh[:, gate(2)])
        )
        hold = hs[:, here].astype(F32)
        change = (1.0 - update) * (fresh - hold)
        hn[:, here] = hold + change
        delta = mm(src_hot_t, change.astype(BF16))
        for k in range(2):
            dsend[2 * c + k] = (delta[:, k * LANES:(k + 1) * LANES] * share).astype(BF16)
        if not sent:
            delta_copy(line(2)).start()
            delta_copy(4 * c + 1 - line(2)).start()
        else:
            delta_copy(4 * c + 1 - r).start()
        sent.append(c)

    dall[r] = dsend[r]
    for i in range(1, m):
        finish(dall.at[0], delta_sem.at[1, line(i)])

    def post(turn, to):
        remote(outbuf.at[to], landed.at[s], out_sem, (turn,), to, r).start()

    span = 2 * W * G
    for turn in turns:
        first = quarter(turn) * 2 * W
        part = mm(place_hot[pl.ds(pl.multiple_of(first * G, span), span)], dall[...].reshape(m * T, LANES))
        outbuf[pl.ds(first, 2 * W)] = part.astype(BF16).reshape(2 * W, G, LANES)
        if turn == turns[0]:
            scatter(first_lines, post)
    scatter(other_lines, post)
    give(groups[1])
    landed[s] = outbuf[s]

    for i in range(1, m):
        finish(asked_all.at[0], ask_sem.at[1, i])
    fan_no = jnp.floor((iota((n, n * G), 1).astype(F32) + 0.5) * (1.0 / G))
    fan = one_hot(fan_no == iota((n, n * G), 0).astype(F32))
    lane_no = iota((2 * PAD, n * G), 1).astype(F32)
    seat = lane_no - jnp.floor((lane_no + 0.5) * (1.0 / G)) * float(G)
    line_no = iota((2 * PAD, n * G), 0)
    weight = jnp.where(line_no < PAD, 32.0, 1.0)
    seat_of = (line_no & (PAD - 1)).astype(F32)
    target = jnp.full((1, n * G), -1.0, F32)
    for q in range(m):
        turned = jnp.transpose(asked_all[q])[:2 * PAD].astype(BF16)
        values = mm(turned, fan) * weight
        here = (seat == seat_of + float(q * cap)) & (seat_of < float(cap))
        target = target + jnp.sum(jnp.where(here, values, 0.0), axis=0, keepdims=True)
    step = LANES

    def fill_owner(c, carry):
        at = pl.multiple_of(c * step, step)
        owner_hot[pl.ds(at, step)] = one_hot((iota((step, n * G), 0) + c * step).astype(F32) == target)
        return carry

    lax.fori_loop(0, R // step, fill_owner, 0)

    arrive(groups[1])
    others(groups[1], lambda ref, w, i: finish(ref, wc_sem.at[1, w, i]))
    query = mm(hn[...].astype(BF16), wq[...]).astype(BF16)
    keyval = mm(hd[...], wk[...]).astype(BF16)
    head = D // H
    blocks = E // BLK
    block_no = iota((BLK, E), 1) >> 7
    for q in range(blocks):
        times = sum((block_no == listed_ref[k:k + 1, q:q + 1]).astype(F32) for k in range(2))
        seen = times > 0.0
        for h in range(H):
            cols = slice(h * head, (h + 1) * head)
            at = slice(q * BLK, (q + 1) * BLK)
            scores = mm_nt(query[at, cols], keyval[:, cols]) * (1.0 / math.sqrt(head))
            scores = jnp.where(seen, scores, -jnp.inf)
            top = jnp.max(scores, axis=1, keepdims=True)
            weighed = jnp.exp(scores - top) * times
            prob = (weighed / jnp.sum(weighed, axis=1, keepdims=True)).astype(BF16)
            attend = mm(prob, keyval[:, D + h * head:D + (h + 1) * head])
            embed_ref[at, cols] = (hn[at, cols] + attend).astype(BF16)

    embed_copy = pltpu.make_async_copy(embed_ref, embed_hbm, local_sem.at[1])
    embed_copy.start()

    def cols_of(rep):
        return pl.ds(pl.multiple_of(rep * LANES, LANES), LANES)

    def landed_part(turn, lines):
        first = quarter(half - turn) * 2 * W
        hot = owner_hot[lines, pl.ds(pl.multiple_of(first * G, span), span)]
        return mm(hot, landed[pl.ds(first, 2 * W)].reshape(span, LANES))

    right, left = line(1), line(m - 1)
    for turn in turns[:-1]:
        finish(landed.at[pl.ds(0, group_size(turn))], out_sem.at[1, turn])
        part = landed_part(turn, slice(None))
        total[...] = part if turn == turns[0] else total[...] + part
    turn = turns[-1]
    finish(landed.at[pl.ds(0, group_size(turn))], out_sem.at[1, turn])
    step = R // CUTS

    def new_copy(kind, c, src, owner_rep, to):
        at = (pl.ds(c * step, step), cols_of(owner_rep))
        return remote(new_ref.at[at] if src is None else src, new_ref.at[at], new_sem, (kind, c), s, to)

    for c in range(CUTS):
        at = pl.ds(c * step, step)
        newcol[at] = (mem[at, cols_of(r)].astype(F32) + (total[at] + landed_part(turn, at))).astype(BF16)
        new_copy(0, c, newcol.at[at], r, right).start()
        new_copy(1, c, newcol.at[at], r, left).start()
    keep = pltpu.make_async_copy(newcol, new_ref.at[:, cols_of(r)], local_sem.at[0])
    keep.start()
    for c in range(CUTS):
        if c % 2 == 0:
            finish(newcol.at[pl.ds(0, step)], new_sem.at[1, 0, c])
            new_copy(2, c, None, left, right).start()
        else:
            finish(newcol.at[pl.ds(0, step)], new_sem.at[1, 1, c])
            new_copy(3, c, None, right, left).start()
    keep.wait()
    for c in range(CUTS):
        finish(newcol.at[pl.ds(0, step)], new_sem.at[1, 1 - c % 2, c])
        finish(newcol.at[pl.ds(0, step)], new_sem.at[1, 2 + c % 2, c])

    embed_copy.wait()
    finish(halfway.at[pl.ds(0, YS - 1)], req_sem.at[0, 0])
    finish(asked.at[:, pl.ds(0, W - 1)], req_sem.at[0, 1])
    for turn in turns:
        finish(rows.at[pl.ds(0, group_size(turn)), pl.ds(0, cap)], row_sem.at[0, turn])
        finish(landed.at[pl.ds(0, group_size(turn))], out_sem.at[0, turn])
    for c in range(CUTS):
        for kind in (0, 1, 2 + c % 2):
            finish(newcol.at[pl.ds(0, step)], new_sem.at[0, kind, c])
    for i in range(1, m):
        finish(slots_all.at[0], slot_sem.at[0, i])
        finish(asked_all.at[0], ask_sem.at[0, i])
        finish(dall.at[0], delta_sem.at[0, line(i)])
    for g in range(2):
        others(groups[g], lambda ref, w, i: finish(ref, wx_sem.at[0, w, i]))
        others(groups[g], lambda ref, w, i: finish(ref, wc_sem.at[0, w, i]))


def settle(embed_in, new_in, embed_out, new_out, embed_buf, new_buf, sems):
    moves = []
    for src, buf, dst, count in ((new_in, new_buf, new_out, 4), (embed_in, embed_buf, embed_out, 2)):
        size = src.shape[0] // count
        for c in range(count):
            at = pl.ds(c * size, size)
            k = len(moves)
            moves.append((
                pltpu.make_async_copy(src.at[at], buf.at[at], sems.at[0, k]),
                pltpu.make_async_copy(buf.at[at], dst.at[at], sems.at[1, k]),
            ))
            moves[-1][0].start()
    for come, go in moves:
        come.wait()
        go.start()
    for come, go in moves:
        go.wait()


def shards(
    memory, touch_owner, touch_row, touch_time, src_slot, dst_slot, event_time, neighbour_blocks,
    time_freq, time_phase, w_input, w_time, w_hidden, w_query, w_keyval,
):
    n = lax.axis_size("shard")
    m = lax.axis_size("rep")
    T = touch_row.shape[0]
    E = src_slot.shape[0]
    R, D = memory.shape
    cap = 2 * T // n + 2
    G = m * cap
    anywhere = pl.BlockSpec(memory_space=pl.ANY)
    weights = (w_input, w_time, w_hidden, w_query, w_keyval)
    dma = pltpu.SemaphoreType.DMA
    small = (
        touch_owner.reshape(1, T), touch_row.reshape(1, T), touch_time.reshape(1, T),
        src_slot, dst_slot, event_time,
        neighbour_blocks.T, time_freq.reshape(1, -1), time_phase.reshape(1, -1),
    )
    embed, new_memory = pl.pallas_call(
        functools.partial(body, n, m, cap),
        out_shape=(jax.ShapeDtypeStruct((E, D), BF16), jax.ShapeDtypeStruct((R, D), BF16)),
        in_specs=[anywhere] * 15,
        out_specs=(anywhere, anywhere),
        scratch_shapes=[pltpu.VMEM(x.shape, x.dtype) for x in small]
        + [dma((len(small),)), pltpu.VMEM((E, D), BF16), pltpu.VMEM((R, D), BF16)]
        + [pltpu.VMEM((w.shape[0], w.shape[1] * m), BF16) for w in weights]
        + [
            pltpu.VMEM((YS, n // YS, 1, LANES), F32),
            pltpu.VMEM((YS, n // YS, 1, LANES), F32),
            pltpu.VMEM((YS, n // YS, 1, LANES), F32),
            pltpu.VMEM((m, n, LANES), F32),
            pltpu.VMEM((m, 1, T), F32),
            pltpu.VMEM((n, PAD, D), BF16),
            pltpu.VMEM((n, PAD, D), BF16),
            pltpu.VMEM((n * G, m * T), BF16),
            pltpu.VMEM((R, n * G), BF16),
            pltpu.VMEM((E, D), BF16),
            pltpu.VMEM((E, D), BF16),
            pltpu.VMEM((E, D), F32),
            pltpu.VMEM((m, T, LANES), BF16),
            pltpu.VMEM((m, T, LANES), BF16),
            pltpu.VMEM((n, G, LANES), BF16),
            pltpu.VMEM((n, G, LANES), BF16),
            pltpu.VMEM((R, LANES), BF16),
            pltpu.VMEM((T, n * PAD), BF16),
            pltpu.VMEM((R, LANES), F32),
            dma((6,)),
            dma((2, 2)),
            dma((2, m)),
            dma((2, m)),
            dma((2, len(weights), m)),
            dma((2, len(weights), m)),
            dma((2, YS // 2)),
            dma((2, m)),
            dma((2, YS // 2)),
            dma((2, 4, CUTS)),
        ],
        compiler_params=pltpu.CompilerParams(
            collective_id=0, has_side_effects=True, vmem_limit_bytes=56 * 1024 * 1024
        ),
    )(
        *small,
        memory, *weights,
    )
    return pl.pallas_call(
        settle,
        out_shape=(jax.ShapeDtypeStruct((E, D), BF16), jax.ShapeDtypeStruct((R, D), BF16)),
        in_specs=[anywhere] * 2,
        out_specs=(anywhere, anywhere),
        scratch_shapes=[pltpu.VMEM((E, D), BF16), pltpu.VMEM((R, D), BF16), dma((2, 6))],
        cost_estimate=pl.CostEstimate(flops=0, bytes_accessed=4 * (E + R) * D, transcendentals=0),
    )(embed, new_memory)


def solution(mesh):
    both = P(("shard", "rep"))
    placed = (
        P("shard", None), P(("shard", "rep"), None), both, both, both, both, both,
        P(("shard", "rep"), None), P(), P(),
    ) + (P(None, "rep"),) * 5
    return jax.shard_map(
        shards,
        mesh=mesh,
        in_specs=placed,
        out_specs=(P(("shard", "rep"), None), P("shard", None)),
        check_vma=False,
    )
```
